128 devices in a mesh: planes: 16 (over x, z), rows: 8 (over y, core).
Axes of the slice: x: 4, y: 4, z: 4, core: 2. Of those that a mesh axis runs over, the one named last changes fastest.
Arguments:
- movie: bfloat16 [262144, 2048], P(('planes', 'rows')), may hold values from -6 to 6
- entry_tile: int32 [262144], P(('planes', 'rows')), may hold values from 0 to 2047
- entry_neuron: int32 [262144], P(('planes', 'rows')), may hold values from 0 to 98303, as said below
- entry_weights: bfloat16 [262144, 128], P(('planes', 'rows')), may hold values from 0 to 0.1796875
- intersection_self: float32 [98304, 768], P(('planes', 'rows'))
- intersection_prev: float32 [98304, 768], P(('planes', 'rows')), may hold values from -0.0625 to 0.0625
- intersection_next: float32 [98304, 768], P(('planes', 'rows')), may hold values from -0.0625 to 0.0625
- prev_traces: float32 [16, 98304], P(None, ('planes', 'rows')), may hold values from 0 to 2
Outputs:
- traces: float32 [16, 98304], P(None, ('planes', 'rows'))
The draws below stay inside these ranges and needn't reach their ends.
Inputs may be any that keep to these rules, and one draw needn't show every extreme that they name: `entry_neuron`: the footprint tiles of one device come in groups of 32 consecutive entries; all entries of one group name neurons of one neuron block (neuron // 768); the first group of each device names the device's own block, and the groups of one device name distinct blocks.
All inputs are finite; a program needn't handle non-finite values.
Results may differ from the reference program's by a relative error of at most 0.0003.
Values sent between devices are 32-bit elements; how exact they have to be, the bound alone decides.
No kernel may reach another device: no remote copies, remote signals or barrier semaphores. Data moves between devices by JAX's collectives and lax.ppermute only.
A program may use at most 192 MiB of HBM per device.

```python
import jax
import jax.numpy as jnp
from jax import lax

FRAMES = 16
TILE_VOX = 128
TILE_DEV = 2048
ENT_DEV = 2048
NEUR_DEV = 768
SWEEPS = 3
TILES = 262144
ENTRIES = 262144
NEUR = 98304
CAP = 32
N_PLANES = 16
N_ROWS = 8


def draw_entry_neuron(key, part):
    devices = NEUR // NEUR_DEV
    groups = ENT_DEV // CAP

    def one_device(owner):
        order = jax.random.permutation(jax.random.fold_in(key, owner), devices - 1)
        others = (owner + 1 + order) % devices
        return jnp.concatenate([owner[None], others[:groups - 1]])
    owners = jnp.arange(devices, dtype=jnp.int32)
    targets = jax.vmap(one_device)(owners)
    inside = jax.random.randint(jax.random.fold_in(key, 7777), (devices, groups, CAP), 0, NEUR_DEV)
    neurons = targets[:, :, None] * NEUR_DEV + inside
    return neurons.reshape(ENTRIES).astype(jnp.int32)


def draw_intersection_self(key, part):
    spread = (12.0 * NEUR_DEV) ** (-0.5)
    key_off, key_diag = jax.random.split(key)
    off = jax.random.normal(key_off, (NEUR, NEUR_DEV), jnp.float32) * spread
    own = jax.random.uniform(key_diag, (NEUR, NEUR_DEV), jnp.float32, 1.0, 1.8)
    row_index = jnp.arange(NEUR, dtype=jnp.int32)[:, None] % NEUR_DEV
    col_index = jnp.arange(NEUR_DEV, dtype=jnp.int32)[None, :]
    return jnp.where(row_index == col_index, own, off).astype(jnp.float32)


def set_ends(entries, rng, smallest, top_value):
    longest = entries.shape.index(max(entries.shape))
    spots = []
    for shift in (0, 1):
        where = [jax.random.randint(jax.random.fold_in(rng, axis), (), 0, length) for axis, length in enumerate(entries.shape)]
        where[longest] = (where[longest] + shift) % entries.shape[longest]
        spots.append(tuple(where))
    return entries.at[spots[0]].set(smallest).at[spots[1]].set(top_value)


def block_levels(own_key, shape, cuts, least, largest):
    loudness = 1.0
    for position, parts in cuts:
        draws = jax.random.uniform(jax.random.fold_in(jax.random.fold_in(own_key, 6), position), (parts,), jnp.float32, least / len(cuts), largest / len(cuts))
        loudness = loudness * jnp.repeat(jnp.exp(draws), shape[position] // parts).reshape((-1,) + (1,) * (len(shape) - 1 - position))
    return loudness


def gaussian(own_key, extent, scale, most, shards=(), kind=jnp.bfloat16):
    array = jax.random.normal(own_key, extent, jnp.float32) * scale
    if len(shards) > 0:
        array = block_levels(own_key, extent, shards, -0.22, 0.18) * array
    return jnp.clip(array, min=-most, max=most).astype(kind)


def setup_inputs(seed: int = 0) -> dict:
    key_list = jax.random.split(jax.random.key(seed), 9)
    movie = gaussian(key_list[0], (TILES, FRAMES * TILE_VOX), 1.0, 6.0, ((0, 128),))
    entry_tile = set_ends(jax.random.randint(key_list[1], (ENTRIES,), 0, TILE_DEV), jax.random.fold_in(key_list[1], 1), 0, TILE_DEV - 1).astype(jnp.int32)
    entry_neuron = draw_entry_neuron(jax.random.fold_in(key_list[8], 71), 0)
    entry_weights = jnp.clip(0.1796875 * jax.random.uniform(key_list[3], (ENTRIES, TILE_VOX), jnp.float32) ** block_levels(key_list[3], (ENTRIES, TILE_VOX), ((0, 128),), -0.2, 0.2), 0.0, 0.1796875).astype(jnp.bfloat16)
    intersection_self = draw_intersection_self(jax.random.fold_in(key_list[8], 71), 0)
    intersection_prev = gaussian(key_list[5], (NEUR, NEUR_DEV), (12 * NEUR_DEV) ** -0.5, 0.0625, ((0, 128),), jnp.float32)
    intersection_next = gaussian(key_list[6], (NEUR, NEUR_DEV), (12 * NEUR_DEV) ** -0.5, 0.0625, ((0, 128),), jnp.float32)
    prev_traces = jnp.clip(2.0 * jax.random.uniform(key_list[7], (FRAMES, NEUR), jnp.float32) ** block_levels(key_list[7], (FRAMES, NEUR), ((1, 128),), -0.2, 0.2), 0.0, 2.0)
    return {"movie": movie, "entry_tile": entry_tile, "entry_neuron": entry_neuron, "entry_weights": entry_weights, "intersection_self": intersection_self, "intersection_prev": intersection_prev, "intersection_next": intersection_next, "prev_traces": prev_traces}


def reference(movie, entry_tile, entry_neuron, entry_weights, intersection_self, intersection_prev, intersection_next, prev_traces):
    devices = N_PLANES * N_ROWS
    slabs = movie.reshape(devices, TILE_DEV, FRAMES * TILE_VOX)
    tiles_of = entry_tile.reshape(devices, ENT_DEV)
    weights_of = entry_weights.reshape(devices, ENT_DEV, TILE_VOX)

    def one_device(packed):
        slab, tiles, weights = packed
        picked = slab[tiles].reshape(ENT_DEV, FRAMES, TILE_VOX).astype(jnp.float32)
        return jnp.einsum("efv,ev->ef", picked, weights.astype(jnp.float32))

    contrib = lax.map(one_device, (slabs, tiles_of, weights_of)).reshape(ENTRIES, FRAMES)
    projected = jnp.zeros((NEUR, FRAMES), jnp.float32).at[entry_neuron].add(contrib).T
    self_blocks = intersection_self.reshape(devices, NEUR_DEV, NEUR_DEV)
    prev_blocks = intersection_prev.reshape(devices, NEUR_DEV, NEUR_DEV)
    next_blocks = intersection_next.reshape(devices, NEUR_DEV, NEUR_DEV)
    diagonal = jnp.diagonal(self_blocks, axis1=1, axis2=2).reshape(NEUR)
    hp = lax.Precision.HIGHEST
    current = prev_traces
    for sweep in range(SWEEPS):
        blocks = current.reshape(FRAMES, devices, NEUR_DEV)
        empty = jnp.zeros_like(blocks[:, :1])
        before = jnp.concatenate([empty, blocks[:, :-1]], axis=1)
        after = jnp.concatenate([blocks[:, 1:], empty], axis=1)
        coupled = jnp.einsum("fdj,dji->fdi", blocks, self_blocks, precision=hp)
        coupled = coupled + jnp.einsum("fdj,dji->fdi", before, prev_blocks, precision=hp)
        coupled = coupled + jnp.einsum("fdj,dji->fdi", after, next_blocks, precision=hp)
        coupled = coupled.reshape(FRAMES, NEUR)
        current = jnp.maximum(current + (projected - coupled) / diagonal, 0.0)
    return current
```

```python
import jax
import jax.numpy as jnp
from jax import lax
from jax.experimental import pallas as pl
from jax.experimental.pallas import tpu as pltpu
from jax.sharding import PartitionSpec as P

SWEEPS = 3
AXES = ("planes", "rows")
LANES = 128
CAP = 32
SLOT = 5
CHUNKS = 8


def from_behind(block, distance):
    devices = range(lax.axis_size(AXES))
    route = [(i - distance, i) for i in devices if i - distance in devices]
    return lax.ppermute(block, AXES, route)


def swap_blocks(x):
    row = lax.broadcasted_iota(jnp.int32, x.shape, 0) // 4
    col = lax.broadcasted_iota(jnp.int32, x.shape, 1) // CAP
    out = x
    for d in range(1, 4):
        moved = pltpu.roll(pltpu.roll(x, CAP * d, 1), 16 - 4 * d, 0)
        out = jnp.where((col - row) % 4 == d, moved, out)
    return out


def contrib_kernel(tile_ref, neuron_ref, movie_ref, weight_ref, names_ref, out_ref, raw, slab, wide, sem):
    rows = movie_ref.shape[0] // CHUNKS

    def fetch(c):
        return pltpu.make_async_copy(movie_ref.at[pl.ds(c * rows, rows)], raw.at[c], sem.at[c])

    for c in range(CHUNKS):
        fetch(c).start()
    out_ref[...] = jnp.zeros_like(out_ref)
    for c in range(CHUNKS):
        fetch(c).wait()

        @pl.loop(0, rows // 16)
        def _(r):
            base = pl.multiple_of((c * rows + r * 16) * 16, 256)
            for f in range(16):
                x = raw[c, pl.ds(pl.multiple_of(r * 16, 16), 16), pl.ds(f * LANES, LANES)].astype(jnp.float32)
                slab[pl.ds(base + f * 8, 8), :] = x[:8]
                slab[pl.ds(base + 128 + f * 8, 8), :] = x[8:]

    lane = lax.broadcasted_iota(jnp.int32, (16, LANES), 1)

    @pl.loop(0, tile_ref.shape[0] // LANES)
    def _(b):
        start = pl.multiple_of(b * LANES, LANES)
        wide[...] = weight_ref[pl.ds(start, LANES), :].astype(jnp.float32)
        acc = jnp.zeros((16, LANES), jnp.float32)
        for e in range(LANES):
            t = tile_ref[start + e]
            at = (t // 8) * 128 + t % 8
            x = slab[pl.ds(at, 16, stride=8), :]
            s = jnp.sum(x * wide[pl.ds(e, 1), :], axis=1, keepdims=True)
            acc = jnp.where(lane == e, s, acc)
        slots = swap_blocks(acc)
        names = swap_blocks(jnp.broadcast_to(names_ref[pl.ds(b, 1), :].astype(jnp.float32), (16, LANES)))
        for g in range(4):
            owner = neuron_ref[start + g * CAP] // 768
            out_ref[pl.ds(owner * SLOT, 4), :] = slots[4 * g : 4 * g + 4]
            out_ref[pl.ds(owner * SLOT + 4, 1), :] = names[4 * g : 4 * g + 1]


def contributions(movie, entry_tile, entry_neuron, entry_weights, devices):
    tiles = movie.shape[0]
    entries = entry_tile.shape[0]
    return pl.pallas_call(
        contrib_kernel,
        out_shape=jax.ShapeDtypeStruct((devices * SLOT, LANES), jnp.float32),
        grid_spec=pltpu.PrefetchScalarGridSpec(
            num_scalar_prefetch=2,
            grid=(1,),
            in_specs=[
                pl.BlockSpec(memory_space=pl.ANY),
                pl.BlockSpec((entries, LANES), lambda i, *_: (0, 0)),
                pl.BlockSpec((entries // LANES, LANES), lambda i, *_: (0, 0)),
            ],
            out_specs=pl.BlockSpec((devices * SLOT, LANES), lambda i, *_: (0, 0)),
            scratch_shapes=[
                pltpu.VMEM((CHUNKS, tiles // CHUNKS, movie.shape[1]), jnp.bfloat16),
                pltpu.VMEM((tiles * 16, LANES), jnp.float32),
                pltpu.VMEM((LANES, LANES), jnp.float32),
                pltpu.SemaphoreType.DMA((CHUNKS,)),
            ],
        ),
        compiler_params=pltpu.CompilerParams(vmem_limit_bytes=40 << 20),
    )(entry_tile, entry_neuron, movie, entry_weights, entry_neuron.reshape(entries // LANES, LANES))


def combine_kernel(me_ref, got_ref, out_ref, left, hot):
    sources = got_ref.shape[0] // SLOT
    first = me_ref[0] * 768
    lane4 = lax.broadcasted_iota(jnp.int32, (1, LANES), 1) // CAP
    sub = lax.broadcasted_iota(jnp.int32, (256, LANES), 0).astype(jnp.float32)

    @pl.loop(0, sources // 4)
    def _(b):
        row = b * 4 * SLOT
        x = jnp.concatenate([got_ref[pl.ds(row + s * SLOT, 4), :] for s in range(4)], axis=0)
        x = swap_blocks(x)
        name = got_ref[pl.ds(row + 4, 1), :]
        for s in range(1, 4):
            name = jnp.where(lane4 == s, got_ref[pl.ds(row + s * SLOT + 4, 1), :], name)
        name = name - first.astype(jnp.float32)
        high = jnp.where(name >= 512.0, 2.0, jnp.where(name >= 256.0, 1.0, 0.0))
        low = name - 256.0 * high
        big = x.astype(jnp.bfloat16).astype(jnp.float32)
        rest = x - big
        at = pl.ds(pl.multiple_of(b * LANES, LANES), LANES)
        for h in range(3):
            here = high == float(h)
            left[pl.ds(h * 32, 16), at] = jnp.where(here, big, 0.0).astype(jnp.bfloat16)
            left[pl.ds(h * 32 + 16, 16), at] = jnp.where(here, rest, 0.0).astype(jnp.bfloat16)
        hot[:, at] = jnp.where(sub == low, 1.0, 0.0).astype(jnp.bfloat16)

    sums = lax.dot_general(left[...], hot[...], (((1,), (1,)), ((), ())), preferred_element_type=jnp.float32)
    for h in range(3):
        out_ref[:, pl.ds(h * 256, 256)] = sums[h * 32 : h * 32 + 16] + sums[h * 32 + 16 : h * 32 + 32]


def combine(me, got):
    sources = got.shape[0] // SLOT
    return pl.pallas_call(
        combine_kernel,
        out_shape=jax.ShapeDtypeStruct((16, 768), jnp.float32),
        in_specs=[pl.BlockSpec(memory_space=pltpu.SMEM), pl.BlockSpec(memory_space=pltpu.VMEM)],
        out_specs=pl.BlockSpec(memory_space=pltpu.VMEM),
        scratch_shapes=[
            pltpu.VMEM((96, sources * CAP), jnp.bfloat16),
            pltpu.VMEM((256, sources * CAP), jnp.bfloat16),
        ],
        compiler_params=pltpu.CompilerParams(vmem_limit_bytes=16 << 20),
    )(me, got)


def local(
    movie,
    entry_tile,
    entry_neuron,
    entry_weights,
    intersection_self,
    intersection_prev,
    intersection_next,
    prev_traces,
):
    devices = lax.axis_size(AXES)
    neur_dev = prev_traces.shape[1]
    me = lax.axis_index(AXES).reshape(1).astype(jnp.int32)
    send = contributions(movie, entry_tile, entry_neuron, entry_weights, devices)
    got = lax.all_to_all(send.reshape(devices, 1, SLOT * LANES), AXES, 0, 0)
    projected = combine(me, got.reshape(devices * SLOT, LANES))
    eye = jnp.arange(neur_dev)[:, None] == jnp.arange(neur_dev)[None, :]
    diagonal = jnp.sum(jnp.where(eye, intersection_self, 0.0), axis=0)
    highest = lax.Precision.HIGHEST
    current = prev_traces
    for sweep in range(SWEEPS):
        before = from_behind(current, 1)
        after = from_behind(current, -1)
        coupled = jnp.dot(current, intersection_self, precision=highest)
        coupled = coupled + jnp.dot(before, intersection_prev, precision=highest)
        coupled = coupled + jnp.dot(after, intersection_next, precision=highest)
        current = jnp.maximum(current + (projected - coupled) / diagonal, 0.0)
    return current


def solution(mesh):
    return jax.shard_map(
        local,
        mesh=mesh,
        in_specs=(
            P(AXES, None),
            P(AXES),
            P(AXES),
            P(AXES, None),
            P(AXES, None),
            P(AXES, None),
            P(AXES, None),
            P(None, AXES),
        ),
        out_specs=P(None, AXES),
        check_vma=False,
    )
```

```python
import jax
import jax.numpy as jnp
from jax import lax
from jax.experimental import pallas as pl
from jax.experimental.pallas import tpu as pltpu
from jax.sharding import PartitionSpec as P

SWEEPS = 3
AXES = ("planes", "rows")
LANES = 128
CAP = 32
SLOT = 5
PREPARE_MB = 50
PITCH = 9
WIDE = 256
PARTS = 8
PIECE = WIDE // PARTS
HBM = pl.BlockSpec(memory_space=pltpu.HBM)
VMEM = pl.BlockSpec(memory_space=pltpu.VMEM)


def place():
    return lax.axis_index(AXES)


def update(coupled, c, projected, diag):
    return jnp.maximum(c + (projected - coupled) / diag, 0.0)


def swap_blocks(x):
    row = lax.broadcasted_iota(jnp.int32, x.shape, 0) // 4
    col = lax.broadcasted_iota(jnp.int32, x.shape, 1) // CAP
    out = x
    for d in range(1, 4):
        moved = pltpu.roll(pltpu.roll(x, CAP * d, 1), 16 - 4 * d, 0)
        out = jnp.where((col - row) % 4 == d, moved, out)
    return out


def contrib_kernel(
    movie_ref, tile_hbm, neuron_hbm, weight_hbm,
    out_ref,
    slab, left, fan, weight, tile, neuron, row, row_s, neuron_s, sem2,
):
    group = 16 * PITCH
    small = [
        pltpu.make_async_copy(source, target, sem2.at[i])
        for i, (source, target) in enumerate(
            [
                (tile_hbm, tile),
                (neuron_hbm, neuron),
                (neuron_hbm, neuron_s),
                (weight_hbm, weight),
            ]
        )
    ]
    for copy in small:
        copy.start()
    out_ref[...] = jnp.zeros_like(out_ref)
    for copy in small:
        copy.wait()
    row[...] = (tile[...] >> 3) * group + (tile[...] & 7)
    to_scalar = pltpu.make_async_copy(row, row_s, sem2.at[5])
    to_scalar.start()

    @pl.loop(0, movie_ref.shape[0] // 16, unroll=2)
    def _(r):
        base = r * 2 * group
        for f in range(16):
            x = movie_ref[pl.ds(pl.multiple_of(r * 16, 16), 16), pl.ds(f * LANES, LANES)].astype(jnp.float32)
            slab[pl.ds(base + f * PITCH, 8), :] = x[:8]
            slab[pl.ds(base + group + f * PITCH, 8), :] = x[8:]

    to_scalar.wait()
    fan[...] = jnp.zeros_like(fan)
    eighth = lax.broadcasted_iota(jnp.int32, (16, WIDE), 1) % PIECE

    @pl.loop(0, tile.shape[0] * LANES // WIDE, unroll=tile.shape[0] * LANES // WIDE)
    def _(b):
        start = pl.multiple_of(b * WIDE, WIDE)
        for i in range(PARTS):
            fan[pl.ds(PIECE * i, PIECE), pl.ds(i * LANES, LANES)] = weight[pl.ds(start + PIECE * i, PIECE), :]
        for o in range(PIECE):
            entries = [PIECE * i + o for i in range(PARTS)]
            xs = [
                slab[pl.ds(row_s[2 * b + e // LANES, e % LANES], 16, stride=PITCH), :].astype(jnp.bfloat16)
                for e in entries
            ]
            for i, x in enumerate(xs):
                left[pl.ds(o * 16, 16), pl.ds(i * LANES, LANES)] = x
        every = lax.dot_general(
            left[...], fan[...], (((1,), (1,)), ((), ())), preferred_element_type=jnp.float32
        )
        sums = jnp.zeros((16, WIDE), jnp.float32)
        for o in range(PIECE):
            sums = jnp.where(eighth == o, every[o * 16 : o * 16 + 16], sums)
        for h in range(2):
            slots = swap_blocks(sums[:, h * LANES : (h + 1) * LANES])
            names = neuron[pl.ds(2 * b + h, 1), :].astype(jnp.float32)
            names = swap_blocks(jnp.broadcast_to(names, (16, LANES)))
            for g in range(4):
                owner = lax.div(neuron_s[2 * b + h, g * CAP], 768)
                out_ref[pl.ds(owner * SLOT, 4), :] = slots[4 * g : 4 * g + 4]
                out_ref[pl.ds(owner * SLOT + 4, 1), :] = names[4 * g : 4 * g + 1]


def open_kernel(out_ref):
    out_ref[...] = jnp.zeros_like(out_ref)


def opening():
    return pl.pallas_call(
        open_kernel,
        out_shape=jax.ShapeDtypeStruct((8, LANES), jnp.float32),
        out_specs=VMEM,
        compiler_params=pltpu.CompilerParams(vmem_limit_bytes=1 << 20, has_side_effects=True),
        cost_estimate=pl.CostEstimate(flops=10**10, bytes_accessed=10**7, transcendentals=0),
    )()


def contributions(movie, entry_tile, entry_neuron, entry_weights, devices):
    tiles = movie.shape[0]
    entries = entry_tile.shape[0]
    table = (entries // LANES, LANES)
    return pl.pallas_call(
        contrib_kernel,
        out_shape=jax.ShapeDtypeStruct((devices * SLOT, LANES), jnp.float32),
        in_specs=[VMEM] + [HBM] * 3,
        out_specs=VMEM,
        scratch_shapes=[
            pltpu.VMEM((tiles * 2 * PITCH + 16, LANES), jnp.float32),
            pltpu.VMEM((PIECE * 16, PARTS * LANES), jnp.bfloat16),
            pltpu.VMEM((WIDE, PARTS * LANES), jnp.bfloat16),
            pltpu.VMEM((entries, LANES), jnp.bfloat16),
            pltpu.VMEM(table, jnp.int32),
            pltpu.VMEM(table, jnp.int32),
            pltpu.VMEM(table, jnp.int32),
            pltpu.SMEM(table, jnp.int32),
            pltpu.SMEM(table, jnp.int32),
            pltpu.SemaphoreType.DMA((6,)),
        ],
        compiler_params=pltpu.CompilerParams(vmem_limit_bytes=48 << 20),
        cost_estimate=pl.CostEstimate(flops=10**10, bytes_accessed=10**7, transcendentals=0),
    )(movie, entry_tile.reshape(table), entry_neuron.reshape(table), entry_weights)


def combine_kernel(got_ref, ready_ref, out_ref, first_ref):
    sources = got_ref.shape[0] // SLOT
    first = (place() * 768).astype(jnp.float32)
    lane4 = lax.broadcasted_iota(jnp.int32, (1, LANES), 1) // CAP
    sub = lax.broadcasted_iota(jnp.int32, (256, LANES), 0).astype(jnp.float32)
    sums = jnp.zeros((96, 256), jnp.float32)
    for b in range(sources // 8):
        lefts, hots = [], []
        for i in range(2):
            row = (2 * b + i) * 4 * SLOT
            x = jnp.concatenate([got_ref[row + s * SLOT : row + s * SLOT + 4, :] for s in range(4)], axis=0)
            x = swap_blocks(x)
            name = got_ref[row + 4 : row + 5, :]
            for s in range(1, 4):
                name = jnp.where(lane4 == s, got_ref[row + s * SLOT + 4 : row + s * SLOT + 5, :], name)
            name = name - first
            high = jnp.where(name >= 512.0, 2.0, jnp.where(name >= 256.0, 1.0, 0.0))
            low = name - 256.0 * high
            big = x.astype(jnp.bfloat16).astype(jnp.float32)
            rest = x - big
            both = jnp.concatenate([big, rest], axis=0)
            lefts.append(
                jnp.concatenate([jnp.where(high == float(h), both, 0.0) for h in range(3)], axis=0).astype(jnp.bfloat16)
            )
            hots.append(jnp.where(sub == low, 1.0, 0.0).astype(jnp.bfloat16))
        sums = sums + lax.dot_general(
            jnp.concatenate(lefts, axis=1), jnp.concatenate(hots, axis=1), (((1,), (1,)), ((), ())),
            preferred_element_type=jnp.float32,
        )
    for h in range(3):
        out_ref[:, h * 256 : h * 256 + 256] = sums[h * 32 : h * 32 + 16] + sums[h * 32 + 16 : h * 32 + 32]
    first_ref[...] = update(ready_ref[0:16, :], ready_ref[16:32, :], out_ref[...], ready_ref[32:33, :])


def combine(got, ready):
    out = jax.ShapeDtypeStruct((16, ready.shape[1]), jnp.float32)
    return pl.pallas_call(
        combine_kernel,
        out_shape=(out, out),
        in_specs=[VMEM] * 2,
        out_specs=(VMEM, VMEM),
        compiler_params=pltpu.CompilerParams(vmem_limit_bytes=16 << 20),
        cost_estimate=pl.CostEstimate(flops=10**10, bytes_accessed=10**6, transcendentals=0),
    )(got, ready)


def halves(x):
    big = x.astype(jnp.bfloat16)
    return big, (x - big.astype(jnp.float32)).astype(jnp.bfloat16)


def times(c, high, low):
    big, rest = halves(c)
    main = jnp.dot(jnp.concatenate([big, rest], 0), high, preferred_element_type=jnp.float32)
    minor = jnp.dot(big, low, preferred_element_type=jnp.float32)
    return (minor + main[16:]) + main[:16]


def prepare_kernel(
    c_hbm, a_ref, b_ref, self_hbm, prev_hbm, next_hbm, out_ref, high_ref, low_ref, c, own, close, far, sem
):
    even = place() % 2 == 0

    def fetch(source, target, i):
        return pltpu.make_async_copy(source, target, sem.at[i])

    def fetch_both(close_hbm, far_hbm):
        fetch(close_hbm, close, 2).start()
        fetch(far_hbm, far, 3).start()

    fetch(c_hbm, c, 0).start()
    fetch(self_hbm, own, 1).start()
    pl.when(even)(lambda: fetch_both(next_hbm, prev_hbm))
    pl.when(jnp.logical_not(even))(lambda: fetch_both(prev_hbm, next_hbm))
    fetch(c_hbm, c, 0).wait()
    fetch(self_hbm, own, 1).wait()
    eye = lax.broadcasted_iota(jnp.int32, (LANES, LANES), 0) == lax.broadcasted_iota(jnp.int32, (LANES, LANES), 1)
    for i in range(own.shape[0] // LANES):
        at = pl.ds(i * LANES, LANES)
        diag = jnp.sum(jnp.where(eye, own[at, at], 0.0), axis=0, keepdims=True)
        out_ref[32:40, at] = jnp.broadcast_to(diag, (8, LANES))
    out_ref[16:32, :] = c[...]
    total = times(c[...], *halves(own[...]))
    fetch(next_hbm, close, 2).wait()
    total = total + times(a_ref[...], *halves(close[...]))
    fetch(prev_hbm, far, 3).wait()
    high_ref[...], low_ref[...] = halves(far[...])
    out_ref[0:16, :] = total + times(b_ref[...], high_ref[...], low_ref[...])


def prepare(c, a, b, matrices):
    n = c.shape[1]
    half = jax.ShapeDtypeStruct((n, n), jnp.bfloat16)
    return pl.pallas_call(
        prepare_kernel,
        out_shape=(jax.ShapeDtypeStruct((40, n), jnp.float32), half, half),
        in_specs=[HBM, VMEM, VMEM, HBM, HBM, HBM],
        out_specs=(VMEM,) * 3,
        scratch_shapes=[pltpu.VMEM(c.shape, jnp.float32)]
        + [pltpu.VMEM((n, n), jnp.float32)] * 3
        + [pltpu.SemaphoreType.DMA((4,))],
        compiler_params=pltpu.CompilerParams(vmem_limit_bytes=PREPARE_MB << 20),
        cost_estimate=pl.CostEstimate(flops=5 * 10**9, bytes_accessed=10**7, transcendentals=0),
    )(c, a, b, *matrices)


def near_kernel(c_ref, a_ref, self_ref, prev_ref, next_ref, out_ref):
    own = times(c_ref[...], *halves(self_ref[...]))

    def rest(near_ref):
        out_ref[...] = own + times(a_ref[...], *halves(near_ref[...]))

    even = place() % 2 == 0
    pl.when(even)(lambda: rest(next_ref))
    pl.when(jnp.logical_not(even))(lambda: rest(prev_ref))


def near(c, a, matrices):
    return pl.pallas_call(
        near_kernel,
        out_shape=jax.ShapeDtypeStruct(c.shape, jnp.float32),
        in_specs=[VMEM] * 5,
        out_specs=VMEM,
        compiler_params=pltpu.CompilerParams(vmem_limit_bytes=16 << 20),
        cost_estimate=pl.CostEstimate(flops=5 * 10**8, bytes_accessed=10**6, transcendentals=0),
    )(c, a, *matrices)


def step_kernel(part_ref, b_ref, high_ref, low_ref, c_ref, projected_ref, ready_ref, out_ref):
    far = times(b_ref[...], high_ref[...], low_ref[...])
    out_ref[...] = update(part_ref[...] + far, c_ref[...], projected_ref[...], ready_ref[32:33, :])


def step(part, b, weights, c, projected, ready):
    return pl.pallas_call(
        step_kernel,
        out_shape=jax.ShapeDtypeStruct(c.shape, jnp.float32),
        in_specs=[VMEM] * 7,
        out_specs=VMEM,
        compiler_params=pltpu.CompilerParams(vmem_limit_bytes=16 << 20),
        cost_estimate=pl.CostEstimate(flops=3 * 10**8, bytes_accessed=10**6, transcendentals=0),
    )(part, b, *weights, c, projected, ready)


def exchange(c):
    n = lax.axis_size(AXES)
    a = lax.ppermute(c, AXES, [(i, i ^ 1) for i in range(n)])
    b = lax.ppermute(c, AXES, [(i, i + 1) for i in range(1, n - 1, 2)] + [(i + 1, i) for i in range(1, n - 1, 2)])
    return a, b


def local(
    movie,
    entry_tile,
    entry_neuron,
    entry_weights,
    intersection_self,
    intersection_prev,
    intersection_next,
    prev_traces,
):
    devices = lax.axis_size(AXES)
    matrices = (intersection_self, intersection_prev, intersection_next)
    c, _ = lax.optimization_barrier((prev_traces, opening()))
    a, b = exchange(c)
    here = pltpu.with_memory_space_constraint(movie, pltpu.VMEM)
    send = contributions(here, entry_tile, entry_neuron, entry_weights, devices)
    got = lax.all_to_all(send.reshape(devices, 1, SLOT * LANES), AXES, 0, 0)
    ready, *split = prepare(c, a, b, matrices)
    projected, c = combine(got.reshape(devices * SLOT, LANES), ready)
    for _ in range(SWEEPS - 1):
        a, b = exchange(c)
        part = near(c, a, matrices)
        c = step(part, b, split, c, projected, ready)
    return c


def solution(mesh):
    return jax.shard_map(
        local,
        mesh=mesh,
        in_specs=(
            P(AXES, None),
            P(AXES),
            P(AXES),
            P(AXES, None),
            P(AXES, None),
            P(AXES, None),
            P(AXES, None),
            P(None, AXES),
        ),
        out_specs=P(None, AXES),
        check_vma=False,
    )
```

```python
import jax
import jax.numpy as jnp
from jax import lax
from jax.experimental import pallas as pl
from jax.experimental.pallas import tpu as pltpu
from jax.sharding import PartitionSpec as P

SWEEPS = 3
AXES = ("planes", "rows")
LANES = 128
CAP = 32
SLOT = 9
PREPARE_MB = 50
PITCH = 9
WIDE = 256
PARTS = 8
PIECE = WIDE // PARTS
HBM = pl.BlockSpec(memory_space=pltpu.HBM)
VMEM = pl.BlockSpec(memory_space=pltpu.VMEM)


def place():
    return lax.axis_index(AXES)


def across(block):
    return block + 2 * (block & 1) - 1


def update(coupled, c, projected, diag):
    return jnp.maximum(c + (projected - coupled) / diag, 0.0)


def swap_blocks(x):
    row = lax.broadcasted_iota(jnp.int32, x.shape, 0) // 4
    col = lax.broadcasted_iota(jnp.int32, x.shape, 1) // CAP
    out = x
    for d in range(1, 4):
        moved = pltpu.roll(pltpu.roll(x, CAP * d, 1), 16 - 4 * d, 0)
        out = jnp.where((col - row) % 4 == d, moved, out)
    return out


def contrib_kernel(
    movie_ref, tile_hbm, neuron_hbm, weight_hbm,
    out_ref,
    slab, left, fan, weight, tile, neuron, row, row_s, neuron_s, sem2,
):
    group = 16 * PITCH
    devices = out_ref.shape[0] // SLOT
    small = [
        pltpu.make_async_copy(source, target, sem2.at[i])
        for i, (source, target) in enumerate(
            [
                (tile_hbm, tile),
                (neuron_hbm, neuron),
                (neuron_hbm, neuron_s),
                (weight_hbm, weight),
            ]
        )
    ]
    for copy in small:
        copy.start()
    out_ref[...] = jnp.zeros_like(out_ref)
    for copy in small:
        copy.wait()
    row[...] = (tile[...] >> 3) * group + (tile[...] & 7)
    to_scalar = pltpu.make_async_copy(row, row_s, sem2.at[5])
    to_scalar.start()

    @pl.loop(0, movie_ref.shape[0] // 16, unroll=2)
    def _(r):
        base = r * 2 * group
        for f in range(16):
            x = movie_ref[pl.ds(pl.multiple_of(r * 16, 16), 16), pl.ds(f * LANES, LANES)].astype(jnp.float32)
            slab[pl.ds(base + f * PITCH, 8), :] = x[:8]
            slab[pl.ds(base + group + f * PITCH, 8), :] = x[8:]

    to_scalar.wait()
    fan[...] = jnp.zeros_like(fan)
    eighth = lax.broadcasted_iota(jnp.int32, (16, WIDE), 1) % PIECE

    @pl.loop(0, tile.shape[0] * LANES // WIDE, unroll=tile.shape[0] * LANES // WIDE)
    def _(b):
        start = pl.multiple_of(b * WIDE, WIDE)
        for i in range(PARTS):
            fan[pl.ds(PIECE * i, PIECE), pl.ds(i * LANES, LANES)] = weight[pl.ds(start + PIECE * i, PIECE), :]
        for o in range(PIECE):
            entries = [PIECE * i + o for i in range(PARTS)]
            xs = [
                slab[pl.ds(row_s[2 * b + e // LANES, e % LANES], 16, stride=PITCH), :].astype(jnp.bfloat16)
                for e in entries
            ]
            for i, x in enumerate(xs):
                left[pl.ds(o * 16, 16), pl.ds(i * LANES, LANES)] = x
        every = lax.dot_general(
            left[...], fan[...], (((1,), (1,)), ((), ())), preferred_element_type=jnp.float32
        )
        sums = jnp.zeros((16, WIDE), jnp.float32)
        for o in range(PIECE):
            sums = jnp.where(eighth == o, every[o * 16 : o * 16 + 16], sums)
        for h in range(2):
            slots = swap_blocks(sums[:, h * LANES : (h + 1) * LANES])
            names = neuron[pl.ds(2 * b + h, 1), :].astype(jnp.float32)
            names = swap_blocks(jnp.broadcast_to(names, (16, LANES)))
            for g in range(4):
                owner = lax.div(neuron_s[2 * b + h, g * CAP], 768)
                other = across(owner)
                other = jnp.where((other < 0) | (other >= devices), owner, other)
                for to, half in ((owner, 0), (other, 1)):
                    out_ref[pl.ds(to * SLOT + 4 * half, 4), :] = slots[4 * g : 4 * g + 4]
                    at = pl.ds(half * 64, 64)
                    out_ref[pl.ds(to * SLOT + 8, 1), at] = names[4 * g : 4 * g + 1, half * 64 : half * 64 + 64]


def open_kernel(out_ref):
    out_ref[...] = jnp.zeros_like(out_ref)


def opening():
    return pl.pallas_call(
        open_kernel,
        out_shape=jax.ShapeDtypeStruct((8, LANES), jnp.float32),
        out_specs=VMEM,
        compiler_params=pltpu.CompilerParams(vmem_limit_bytes=1 << 20, has_side_effects=True),
        cost_estimate=pl.CostEstimate(flops=10**10, bytes_accessed=10**7, transcendentals=0),
    )()


def contributions(movie, entry_tile, entry_neuron, entry_weights, devices):
    tiles = movie.shape[0]
    entries = entry_tile.shape[0]
    table = (entries // LANES, LANES)
    return pl.pallas_call(
        contrib_kernel,
        out_shape=jax.ShapeDtypeStruct((devices * SLOT, LANES), jnp.float32),
        in_specs=[VMEM] + [HBM] * 3,
        out_specs=VMEM,
        scratch_shapes=[
            pltpu.VMEM((tiles * 2 * PITCH + 16, LANES), jnp.float32),
            pltpu.VMEM((PIECE * 16, PARTS * LANES), jnp.bfloat16),
            pltpu.VMEM((WIDE, PARTS * LANES), jnp.bfloat16),
            pltpu.VMEM((entries, LANES), jnp.bfloat16),
            pltpu.VMEM(table, jnp.int32),
            pltpu.VMEM(table, jnp.int32),
            pltpu.VMEM(table, jnp.int32),
            pltpu.SMEM(table, jnp.int32),
            pltpu.SMEM(table, jnp.int32),
            pltpu.SemaphoreType.DMA((6,)),
        ],
        compiler_params=pltpu.CompilerParams(vmem_limit_bytes=48 << 20),
        cost_estimate=pl.CostEstimate(flops=10**10, bytes_accessed=10**7, transcendentals=0),
    )(movie, entry_tile.reshape(table), entry_neuron.reshape(table), entry_weights)


def combine_kernel(got_ref, ready_ref, other_ref, out_ref, first_ref, beyond_ref):
    sources = got_ref.shape[0] // SLOT
    me = place()
    blocks = (me, across(me))
    lane = lax.broadcasted_iota(jnp.int32, (1, LANES), 1)
    sub = lax.broadcasted_iota(jnp.int32, (256, LANES), 0).astype(jnp.float32)
    sums = [jnp.zeros((96, 256), jnp.float32)] * 2

    for b in range(sources // 8):
        lefts, hots = ([], []), ([], [])
        for i in range(2):
            row = (2 * b + i) * 4 * SLOT
            r0, r1, r2, r3 = (got_ref[row + s * SLOT + 8 : row + s * SLOT + 9, :] for s in range(4))
            low_pair = jnp.where(lane % 64 < 32, r0, r1)
            high_pair = jnp.where(lane % 64 < 32, r2, r3)
            listed = (
                jnp.where(lane < 64, low_pair, pltpu.roll(high_pair, 64, 1)),
                jnp.where(lane < 64, pltpu.roll(low_pair, 64, 1), high_pair),
            )
            for k in range(2):
                x = jnp.concatenate(
                    [got_ref[row + s * SLOT + 4 * k : row + s * SLOT + 4 * k + 4, :] for s in range(4)], axis=0
                )
                x = swap_blocks(x)
                name = listed[k] - (blocks[k] * 768).astype(jnp.float32)
                high = jnp.where(name >= 512.0, 2.0, jnp.where(name >= 256.0, 1.0, 0.0))
                low = name - 256.0 * high
                big = x.astype(jnp.bfloat16).astype(jnp.float32)
                both = jnp.concatenate([big, x - big], axis=0)
                lefts[k].append(
                    jnp.concatenate([jnp.where(high == float(h), both, 0.0) for h in range(3)], axis=0).astype(jnp.bfloat16)
                )
                hots[k].append(jnp.where(sub == low, 1.0, 0.0).astype(jnp.bfloat16))
        for k in range(2):
            sums[k] = sums[k] + lax.dot_general(
                jnp.concatenate(lefts[k], axis=1), jnp.concatenate(hots[k], axis=1), (((1,), (1,)), ((), ())),
                preferred_element_type=jnp.float32,
            )
    for h in range(3):
        at = pl.ds(h * 256, 256)
        for k, (ref, target) in enumerate([(ready_ref, first_ref), (other_ref, beyond_ref)]):
            projected = sums[k][h * 32 : h * 32 + 16] + sums[k][h * 32 + 16 : h * 32 + 32]
            if k == 0:
                out_ref[:, at] = projected
            target[:, at] = update(ref[0:16, at], ref[16:32, at], projected, ref[32:33, at])

    @pl.when((blocks[1] < 0) | (blocks[1] >= sources))
    def _():
        beyond_ref[...] = jnp.zeros_like(beyond_ref)


def combine(got, ready, other):
    out = jax.ShapeDtypeStruct((16, ready.shape[1]), jnp.float32)
    return pl.pallas_call(
        combine_kernel,
        out_shape=(out,) * 3,
        in_specs=[VMEM] * 3,
        out_specs=(VMEM,) * 3,
        compiler_params=pltpu.CompilerParams(vmem_limit_bytes=16 << 20),
        cost_estimate=pl.CostEstimate(flops=10**10, bytes_accessed=10**6, transcendentals=0),
    )(got, ready, other)


def halves(x):
    big = x.astype(jnp.bfloat16)
    return big, (x - big.astype(jnp.float32)).astype(jnp.bfloat16)


def times(c, high, low):
    big, rest = halves(c)
    main = jnp.dot(jnp.concatenate([big, rest], 0), high, preferred_element_type=jnp.float32)
    minor = jnp.dot(big, low, preferred_element_type=jnp.float32)
    return (minor + main[16:]) + main[:16]


def prepare_kernel(
    c_hbm, a_ref, b_ref, self_hbm, prev_hbm, next_hbm, out_ref, high_ref, low_ref, c, own, close, far, sem
):
    even = place() % 2 == 0

    def fetch(source, target, i):
        return pltpu.make_async_copy(source, target, sem.at[i])

    def fetch_both(close_hbm, far_hbm):
        fetch(close_hbm, close, 2).start()
        fetch(far_hbm, far, 3).start()

    fetch(c_hbm, c, 0).start()
    fetch(self_hbm, own, 1).start()
    pl.when(even)(lambda: fetch_both(next_hbm, prev_hbm))
    pl.when(jnp.logical_not(even))(lambda: fetch_both(prev_hbm, next_hbm))
    fetch(c_hbm, c, 0).wait()
    fetch(self_hbm, own, 1).wait()
    eye = lax.broadcasted_iota(jnp.int32, (LANES, LANES), 0) == lax.broadcasted_iota(jnp.int32, (LANES, LANES), 1)
    for i in range(own.shape[0] // LANES):
        at = pl.ds(i * LANES, LANES)
        diag = jnp.sum(jnp.where(eye, own[at, at], 0.0), axis=0, keepdims=True)
        out_ref[32:40, at] = jnp.broadcast_to(diag, (8, LANES))
    out_ref[16:32, :] = c[...]
    total = times(c[...], *halves(own[...]))
    fetch(next_hbm, close, 2).wait()
    total = total + times(a_ref[...], *halves(close[...]))
    fetch(prev_hbm, far, 3).wait()
    high_ref[...], low_ref[...] = halves(far[...])
    out_ref[0:16, :] = total + times(b_ref[...], high_ref[...], low_ref[...])


def prepare(c, a, b, matrices):
    n = c.shape[1]
    half = jax.ShapeDtypeStruct((n, n), jnp.bfloat16)
    return pl.pallas_call(
        prepare_kernel,
        out_shape=(jax.ShapeDtypeStruct((40, n), jnp.float32), half, half),
        in_specs=[HBM, VMEM, VMEM, HBM, HBM, HBM],
        out_specs=(VMEM,) * 3,
        scratch_shapes=[pltpu.VMEM(c.shape, jnp.float32)]
        + [pltpu.VMEM((n, n), jnp.float32)] * 3
        + [pltpu.SemaphoreType.DMA((4,))],
        compiler_params=pltpu.CompilerParams(vmem_limit_bytes=PREPARE_MB << 20),
        cost_estimate=pl.CostEstimate(flops=5 * 10**9, bytes_accessed=10**7, transcendentals=0),
    )(c, a, b, *matrices)


def near_kernel(c_ref, a_ref, self_ref, prev_ref, next_ref, out_ref):
    own = times(c_ref[...], *halves(self_ref[...]))

    def rest(near_ref):
        out_ref[...] = own + times(a_ref[...], *halves(near_ref[...]))

    even = place() % 2 == 0
    pl.when(even)(lambda: rest(next_ref))
    pl.when(jnp.logical_not(even))(lambda: rest(prev_ref))


def near(c, a, matrices):
    return pl.pallas_call(
        near_kernel,
        out_shape=jax.ShapeDtypeStruct(c.shape, jnp.float32),
        in_specs=[VMEM] * 5,
        out_specs=VMEM,
        compiler_params=pltpu.CompilerParams(vmem_limit_bytes=16 << 20),
        cost_estimate=pl.CostEstimate(flops=5 * 10**8, bytes_accessed=10**6, transcendentals=0),
    )(c, a, *matrices)


def step_kernel(part_ref, b_ref, high_ref, low_ref, c_ref, projected_ref, ready_ref, out_ref):
    far = times(b_ref[...], high_ref[...], low_ref[...])
    out_ref[...] = update(part_ref[...] + far, c_ref[...], projected_ref[...], ready_ref[32:33, :])


def step(part, b, weights, c, projected, ready):
    return pl.pallas_call(
        step_kernel,
        out_shape=jax.ShapeDtypeStruct(c.shape, jnp.float32),
        in_specs=[VMEM] * 7,
        out_specs=VMEM,
        compiler_params=pltpu.CompilerParams(vmem_limit_bytes=16 << 20),
        cost_estimate=pl.CostEstimate(flops=3 * 10**8, bytes_accessed=10**6, transcendentals=0),
    )(part, b, *weights, c, projected, ready)


def swap_in_chip(c):
    n = lax.axis_size(AXES)
    return lax.ppermute(c, AXES, [(i, i ^ 1) for i in range(n)])


def swap_across(c):
    n = lax.axis_size(AXES)
    return lax.ppermute(c, AXES, [(i, across(i)) for i in range(1, n - 1)])


def local(
    movie,
    entry_tile,
    entry_neuron,
    entry_weights,
    intersection_self,
    intersection_prev,
    intersection_next,
    prev_traces,
):
    devices = lax.axis_size(AXES)
    matrices = (intersection_self, intersection_prev, intersection_next)
    c, _ = lax.optimization_barrier((prev_traces, opening()))
    a, b = swap_in_chip(c), swap_across(c)
    here = pltpu.with_memory_space_constraint(movie, pltpu.VMEM)
    send = contributions(here, entry_tile, entry_neuron, entry_weights, devices)
    got = lax.all_to_all(send.reshape(devices, 1, SLOT * LANES), AXES, 0, 0)
    ready, *split = prepare(c, a, b, matrices)
    other = swap_across(ready)
    projected, c, b = combine(got.reshape(devices * SLOT, LANES), ready, other)
    for sweep in range(1, SWEEPS):
        a = swap_in_chip(c)
        if sweep > 1:
            b = swap_across(c)
        part = near(c, a, matrices)
        c = step(part, b, split, c, projected, ready)
    return c


def solution(mesh):
    return jax.shard_map(
        local,
        mesh=mesh,
        in_specs=(
            P(AXES, None),
            P(AXES),
            P(AXES),
            P(AXES, None),
            P(AXES, None),
            P(AXES, None),
            P(AXES, None),
            P(None, AXES),
        ),
        out_specs=P(None, AXES),
        check_vma=False,
    )
```

```python
import functools

import jax
import jax.numpy as jnp
from jax import lax
from jax.experimental import pallas as pl
from jax.experimental.pallas import tpu as pltpu
from jax.sharding import PartitionSpec as P

SWEEPS = 3
AXES = ("planes", "rows")
LANES = 128
CAP = 32
SLOT = 9
PREPARE_MB = 50
PITCH = 9
WIDE = 256
PARTS = 8
PIECE = WIDE // PARTS
HBM = pl.BlockSpec(memory_space=pltpu.HBM)
VMEM = pl.BlockSpec(memory_space=pltpu.VMEM)


def place():
    return lax.axis_index(AXES)


def across(block):
    return block + 2 * (block & 1) - 1


def update(coupled, c, projected, diag):
    return jnp.maximum(c + (projected - coupled) / diag, 0.0)


def swap_blocks(x):
    row = lax.broadcasted_iota(jnp.int32, x.shape, 0) // 4
    col = lax.broadcasted_iota(jnp.int32, x.shape, 1) // CAP
    out = x
    for d in range(1, 4):
        moved = pltpu.roll(pltpu.roll(x, CAP * d, 1), 16 - 4 * d, 0)
        out = jnp.where((col - row) % 4 == d, moved, out)
    return out


def contrib_kernel(
    movie_ref, tile_hbm, neuron_hbm, weight_hbm,
    out_ref,
    slab, left, fan, weight, tile, neuron, row, row_s, neuron_s, sem2,
):
    group = 16 * PITCH
    devices = out_ref.shape[0] // SLOT
    small = [
        pltpu.make_async_copy(source, target, sem2.at[i])
        for i, (source, target) in enumerate(
            [
                (tile_hbm, tile),
                (neuron_hbm, neuron),
                (neuron_hbm, neuron_s),
                (weight_hbm, weight),
            ]
        )
    ]
    for copy in small:
        copy.start()
    out_ref[...] = jnp.zeros_like(out_ref)
    for copy in small:
        copy.wait()
    row[...] = (tile[...] >> 3) * group + (tile[...] & 7)
    to_scalar = pltpu.make_async_copy(row, row_s, sem2.at[5])
    to_scalar.start()

    @pl.loop(0, movie_ref.shape[0] // 16, unroll=2)
    def _(r):
        base = r * 2 * group
        for f in range(16):
            x = movie_ref[pl.ds(pl.multiple_of(r * 16, 16), 16), pl.ds(f * LANES, LANES)].astype(jnp.float32)
            slab[pl.ds(base + f * PITCH, 8), :] = x[:8]
            slab[pl.ds(base + group + f * PITCH, 8), :] = x[8:]

    to_scalar.wait()
    fan[...] = jnp.zeros_like(fan)
    eighth = lax.broadcasted_iota(jnp.int32, (16, WIDE), 1) % PIECE

    @pl.loop(0, tile.shape[0] * LANES // WIDE, unroll=tile.shape[0] * LANES // WIDE)
    def _(b):
        start = pl.multiple_of(b * WIDE, WIDE)
        for i in range(PARTS):
            fan[pl.ds(PIECE * i, PIECE), pl.ds(i * LANES, LANES)] = weight[pl.ds(start + PIECE * i, PIECE), :]
        for o in range(PIECE):
            entries = [PIECE * i + o for i in range(PARTS)]
            xs = [
                slab[pl.ds(row_s[2 * b + e // LANES, e % LANES], 16, stride=PITCH), :].astype(jnp.bfloat16)
                for e in entries
            ]
            for i, x in enumerate(xs):
                left[pl.ds(o * 16, 16), pl.ds(i * LANES, LANES)] = x
        every = lax.dot_general(
            left[...], fan[...], (((1,), (1,)), ((), ())), preferred_element_type=jnp.float32
        )
        sums = jnp.zeros((16, WIDE), jnp.float32)
        for o in range(PIECE):
            sums = jnp.where(eighth == o, every[o * 16 : o * 16 + 16], sums)
        for h in range(2):
            slots = swap_blocks(sums[:, h * LANES : (h + 1) * LANES])
            names = neuron[pl.ds(2 * b + h, 1), :].astype(jnp.float32)
            names = swap_blocks(jnp.broadcast_to(names, (16, LANES)))
            for g in range(4):
                owner = lax.div(neuron_s[2 * b + h, g * CAP], 768)
                other = across(owner)
                other = jnp.where((other < 0) | (other >= devices), owner, other)
                for to, half in ((owner, 0), (other, 1)):
                    out_ref[pl.ds(to * SLOT + 4 * half, 4), :] = slots[4 * g : 4 * g + 4]
                    at = pl.ds(half * 64, 64)
                    out_ref[pl.ds(to * SLOT + 8, 1), at] = names[4 * g : 4 * g + 1, half * 64 : half * 64 + 64]


def open_kernel(out_ref):
    out_ref[...] = jnp.zeros_like(out_ref)


def opening():
    return pl.pallas_call(
        open_kernel,
        out_shape=jax.ShapeDtypeStruct((8, LANES), jnp.float32),
        out_specs=VMEM,
        compiler_params=pltpu.CompilerParams(vmem_limit_bytes=1 << 20, has_side_effects=True),
        cost_estimate=pl.CostEstimate(flops=10**10, bytes_accessed=10**7, transcendentals=0),
    )()


def contributions(movie, entry_tile, entry_neuron, entry_weights, devices):
    tiles = movie.shape[0]
    entries = entry_tile.shape[0]
    table = (entries // LANES, LANES)
    return pl.pallas_call(
        contrib_kernel,
        out_shape=jax.ShapeDtypeStruct((devices * SLOT, LANES), jnp.float32),
        in_specs=[VMEM] + [HBM] * 3,
        out_specs=VMEM,
        scratch_shapes=[
            pltpu.VMEM((tiles * 2 * PITCH + 16, LANES), jnp.float32),
            pltpu.VMEM((PIECE * 16, PARTS * LANES), jnp.bfloat16),
            pltpu.VMEM((WIDE, PARTS * LANES), jnp.bfloat16),
            pltpu.VMEM((entries, LANES), jnp.bfloat16),
            pltpu.VMEM(table, jnp.int32),
            pltpu.VMEM(table, jnp.int32),
            pltpu.VMEM(table, jnp.int32),
            pltpu.SMEM(table, jnp.int32),
            pltpu.SMEM(table, jnp.int32),
            pltpu.SemaphoreType.DMA((6,)),
        ],
        compiler_params=pltpu.CompilerParams(vmem_limit_bytes=48 << 20),
        cost_estimate=pl.CostEstimate(flops=10**10, bytes_accessed=10**7, transcendentals=0),
    )(movie, entry_tile.reshape(table), entry_neuron.reshape(table), entry_weights)


def gathered(half, block, got_ref, out_ref):
    sources = got_ref.shape[0] // SLOT
    lane = lax.broadcasted_iota(jnp.int32, (1, LANES), 1)
    sub = lax.broadcasted_iota(jnp.int32, (256, LANES), 0).astype(jnp.float32)
    sums = jnp.zeros((96, 256), jnp.float32)
    for b in range(sources // 8):
        lefts, hots = [], []
        for i in range(2):
            row = (2 * b + i) * 4 * SLOT
            r0, r1, r2, r3 = (got_ref[row + s * SLOT + 8 : row + s * SLOT + 9, :] for s in range(4))
            pairs = [jnp.where(lane % 64 < 32, r0, r1), jnp.where(lane % 64 < 32, r2, r3)]
            pairs[1 - half] = pltpu.roll(pairs[1 - half], 64, 1)
            name = jnp.where(lane < 64, *pairs) - (block * 768).astype(jnp.float32)
            x = jnp.concatenate(
                [got_ref[row + s * SLOT + 4 * half : row + s * SLOT + 4 * half + 4, :] for s in range(4)], axis=0
            )
            x = swap_blocks(x)
            high = jnp.where(name >= 512.0, 2.0, jnp.where(name >= 256.0, 1.0, 0.0))
            low = name - 256.0 * high
            big = x.astype(jnp.bfloat16).astype(jnp.float32)
            both = jnp.concatenate([big, x - big], axis=0)
            lefts.append(
                jnp.concatenate([jnp.where(high == float(h), both, 0.0) for h in range(3)], axis=0).astype(jnp.bfloat16)
            )
            hots.append(jnp.where(sub == low, 1.0, 0.0).astype(jnp.bfloat16))
        sums = sums + lax.dot_general(
            jnp.concatenate(lefts, axis=1), jnp.concatenate(hots, axis=1), (((1,), (1,)), ((), ())),
            preferred_element_type=jnp.float32,
        )
    for h in range(3):
        out_ref[:, h * 256 : h * 256 + 256] = sums[h * 32 : h * 32 + 16] + sums[h * 32 + 16 : h * 32 + 32]


def first_kernel(got_ref, ready_ref, out_ref, first_ref):
    gathered(0, place(), got_ref, out_ref)
    first_ref[...] = update(ready_ref[0:16, :], ready_ref[16:32, :], out_ref[...], ready_ref[32:33, :])


def beyond_kernel(got_ref, own_ref, out_ref):
    gathered(1, across(place()), got_ref, out_ref)


def combine(kernel, got, other, outs):
    out = jax.ShapeDtypeStruct((16, other.shape[1]), jnp.float32)
    return pl.pallas_call(
        kernel,
        out_shape=(out,) * outs,
        in_specs=[VMEM] * 2,
        out_specs=(VMEM,) * outs,
        compiler_params=pltpu.CompilerParams(vmem_limit_bytes=16 << 20),
        cost_estimate=pl.CostEstimate(flops=10**10 if outs > 1 else 10**8, bytes_accessed=10**6, transcendentals=0),
    )(got, other)


def halves(x):
    big = x.astype(jnp.bfloat16)
    return big, (x - big.astype(jnp.float32)).astype(jnp.bfloat16)


def times(c, high, low):
    big, rest = halves(c)
    main = jnp.dot(jnp.concatenate([big, rest], 0), high, preferred_element_type=jnp.float32)
    minor = jnp.dot(big, low, preferred_element_type=jnp.float32)
    return (minor + main[16:]) + main[:16]


def prepare_kernel(
    c_hbm, a_ref, b_ref, self_hbm, prev_hbm, next_hbm, out_ref, high_ref, low_ref, c, own, close, far, sem
):
    even = place() % 2 == 0

    def fetch(source, target, i):
        return pltpu.make_async_copy(source, target, sem.at[i])

    def fetch_both(close_hbm, far_hbm):
        fetch(close_hbm, close, 2).start()
        fetch(far_hbm, far, 3).start()

    fetch(c_hbm, c, 0).start()
    fetch(self_hbm, own, 1).start()
    pl.when(even)(lambda: fetch_both(next_hbm, prev_hbm))
    pl.when(jnp.logical_not(even))(lambda: fetch_both(prev_hbm, next_hbm))
    fetch(c_hbm, c, 0).wait()
    fetch(self_hbm, own, 1).wait()
    eye = lax.broadcasted_iota(jnp.int32, (LANES, LANES), 0) == lax.broadcasted_iota(jnp.int32, (LANES, LANES), 1)
    for i in range(own.shape[0] // LANES):
        at = pl.ds(i * LANES, LANES)
        diag = jnp.sum(jnp.where(eye, own[at, at], 0.0), axis=0, keepdims=True)
        out_ref[32:40, at] = jnp.broadcast_to(diag, (8, LANES))
    out_ref[16:32, :] = c[...]
    total = times(c[...], *halves(own[...]))
    fetch(next_hbm, close, 2).wait()
    total = total + times(a_ref[...], *halves(close[...]))
    fetch(prev_hbm, far, 3).wait()
    high_ref[...], low_ref[...] = halves(far[...])
    out_ref[0:16, :] = total + times(b_ref[...], high_ref[...], low_ref[...])


def prepare(c, a, b, matrices):
    n = c.shape[1]
    half = jax.ShapeDtypeStruct((n, n), jnp.bfloat16)
    return pl.pallas_call(
        prepare_kernel,
        out_shape=(jax.ShapeDtypeStruct((40, n), jnp.float32), half, half),
        in_specs=[HBM, VMEM, VMEM, HBM, HBM, HBM],
        out_specs=(VMEM,) * 3,
        scratch_shapes=[pltpu.VMEM(c.shape, jnp.float32)]
        + [pltpu.VMEM((n, n), jnp.float32)] * 3
        + [pltpu.SemaphoreType.DMA((4,))],
        compiler_params=pltpu.CompilerParams(vmem_limit_bytes=PREPARE_MB << 20),
        cost_estimate=pl.CostEstimate(flops=2 * 10**10, bytes_accessed=10**7, transcendentals=0),
    )(c, a, b, *matrices)


def near_kernel(c_ref, a_ref, self_ref, prev_ref, next_ref, out_ref):
    own = times(c_ref[...], *halves(self_ref[...]))

    def rest(near_ref):
        out_ref[...] = own + times(a_ref[...], *halves(near_ref[...]))

    even = place() % 2 == 0
    pl.when(even)(lambda: rest(next_ref))
    pl.when(jnp.logical_not(even))(lambda: rest(prev_ref))


def near(c, a, matrices):
    return pl.pallas_call(
        near_kernel,
        out_shape=jax.ShapeDtypeStruct(c.shape, jnp.float32),
        in_specs=[VMEM] * 5,
        out_specs=VMEM,
        compiler_params=pltpu.CompilerParams(vmem_limit_bytes=16 << 20),
        cost_estimate=pl.CostEstimate(flops=5 * 10**8, bytes_accessed=10**6, transcendentals=0),
    )(c, a, *matrices)


def step_kernel(part_ref, b_ref, high_ref, low_ref, c_ref, projected_ref, ready_ref, out_ref):
    far = times(b_ref[...], high_ref[...], low_ref[...])
    out_ref[...] = update(part_ref[...] + far, c_ref[...], projected_ref[...], ready_ref[32:33, :])


def second_step_kernel(
    last, part_ref, other_ref, beyond_ref, high_ref, low_ref, c_ref, projected_ref, ready_ref, out_ref
):
    block = across(place())
    b = update(other_ref[0:16, :], other_ref[16:32, :], beyond_ref[...], other_ref[32:33, :])
    row = lax.broadcasted_iota(jnp.int32, b.shape, 0)
    b = jnp.where(row < jnp.where((block < 0) | (block > last), 0, 16), b, 0.0)
    far = times(b, high_ref[...], low_ref[...])
    out_ref[...] = update(part_ref[...] + far, c_ref[...], projected_ref[...], ready_ref[32:33, :])


def step(kernel, *operands):
    return pl.pallas_call(
        kernel,
        out_shape=jax.ShapeDtypeStruct(operands[0].shape, jnp.float32),
        in_specs=[VMEM] * len(operands),
        out_specs=VMEM,
        compiler_params=pltpu.CompilerParams(vmem_limit_bytes=16 << 20),
        cost_estimate=pl.CostEstimate(flops=3 * 10**8, bytes_accessed=10**6, transcendentals=0),
    )(*operands)


def swap_in_chip(c):
    n = lax.axis_size(AXES)
    return lax.ppermute(c, AXES, [(i, i ^ 1) for i in range(n)])


def swap_across(c):
    n = lax.axis_size(AXES)
    return lax.ppermute(c, AXES, [(i, across(i)) for i in range(1, n - 1)])


def local(
    movie,
    entry_tile,
    entry_neuron,
    entry_weights,
    intersection_self,
    intersection_prev,
    intersection_next,
    prev_traces,
):
    devices = lax.axis_size(AXES)
    matrices = (intersection_self, intersection_prev, intersection_next)
    c, _ = lax.optimization_barrier((prev_traces, opening()))
    a, b = swap_in_chip(c), swap_across(c)
    here = pltpu.with_memory_space_constraint(movie, pltpu.VMEM)
    send = contributions(here, entry_tile, entry_neuron, entry_weights, devices)
    got = lax.all_to_all(send.reshape(devices, 1, SLOT * LANES), AXES, 0, 0)
    ready, *split = prepare(c, a, b, matrices)
    other = swap_across(ready)
    got = got.reshape(devices * SLOT, LANES)
    projected, c = combine(first_kernel, got, ready, 2)
    a = swap_in_chip(c)
    beyond, = combine(beyond_kernel, got, projected, 1)
    part = near(c, a, matrices)
    second_step = functools.partial(second_step_kernel, devices - 1)
    c = step(second_step, part, other, beyond, *split, c, projected, ready)
    for _ in range(SWEEPS - 2):
        a, b = swap_in_chip(c), swap_across(c)
        part = near(c, a, matrices)
        c = step(step_kernel, part, b, *split, c, projected, ready)
    return c


def solution(mesh):
    return jax.shard_map(
        local,
        mesh=mesh,
        in_specs=(
            P(AXES, None),
            P(AXES),
            P(AXES),
            P(AXES, None),
            P(AXES, None),
            P(AXES, None),
            P(AXES, None),
            P(None, AXES),
        ),
        out_specs=P(None, AXES),
        check_vma=False,
    )
```

```python
import functools

import jax
import jax.numpy as jnp
from jax import lax
from jax.experimental import pallas as pl
from jax.experimental.pallas import tpu as pltpu
from jax.sharding import PartitionSpec as P

SWEEPS = 3
AXES = ("planes", "rows")
LANES = 128
CAP = 32
SLOT = 9
PREPARE_MB = 50
PITCH = 9
WIDE = 256
PARTS = 8
PIECE = WIDE // PARTS
HBM = pl.BlockSpec(memory_space=pltpu.HBM)
VMEM = pl.BlockSpec(memory_space=pltpu.VMEM)


def place():
    return lax.axis_index(AXES)


def across(block):
    return block + 2 * (block & 1) - 1


def update(coupled, c, projected, diag):
    return jnp.maximum(c + (projected - coupled) / diag, 0.0)


def swap_blocks(x):
    row = lax.broadcasted_iota(jnp.int32, x.shape, 0) // 4
    col = lax.broadcasted_iota(jnp.int32, x.shape, 1) // CAP
    out = x
    for d in range(1, 4):
        moved = pltpu.roll(pltpu.roll(x, CAP * d, 1), 16 - 4 * d, 0)
        out = jnp.where((col - row) % 4 == d, moved, out)
    return out


def contrib_kernel(
    movie_ref, tile_hbm, neuron_hbm, weight_hbm,
    out_ref,
    slab, left, fan, weight, tile, neuron, row, row_s, neuron_s, sem2,
):
    group = 16 * PITCH
    devices = out_ref.shape[0] // SLOT
    small = [
        pltpu.make_async_copy(source, target, sem2.at[i])
        for i, (source, target) in enumerate(
            [
                (tile_hbm, tile),
                (neuron_hbm, neuron),
                (neuron_hbm, neuron_s),
                (weight_hbm, weight),
            ]
        )
    ]
    for copy in small:
        copy.start()
    out_ref[...] = jnp.zeros_like(out_ref)
    for copy in small:
        copy.wait()
    row[...] = (tile[...] >> 3) * group + (tile[...] & 7)
    to_scalar = pltpu.make_async_copy(row, row_s, sem2.at[5])
    to_scalar.start()

    @pl.loop(0, movie_ref.shape[0] // 16, unroll=2)
    def _(r):
        base = r * 2 * group
        for f in range(16):
            x = movie_ref[pl.ds(pl.multiple_of(r * 16, 16), 16), pl.ds(f * LANES, LANES)].astype(jnp.float32)
            slab[pl.ds(base + f * PITCH, 8), :] = x[:8]
            slab[pl.ds(base + group + f * PITCH, 8), :] = x[8:]

    to_scalar.wait()
    fan[...] = jnp.zeros_like(fan)
    eighth = lax.broadcasted_iota(jnp.int32, (16, WIDE), 1) % PIECE

    @pl.loop(0, tile.shape[0] * LANES // WIDE, unroll=tile.shape[0] * LANES // WIDE)
    def _(b):
        start = pl.multiple_of(b * WIDE, WIDE)
        for i in range(PARTS):
            fan[pl.ds(PIECE * i, PIECE), pl.ds(i * LANES, LANES)] = weight[pl.ds(start + PIECE * i, PIECE), :]
        for o in range(PIECE):
            entries = [PIECE * i + o for i in range(PARTS)]
            xs = [
                slab[pl.ds(row_s[2 * b + e // LANES, e % LANES], 16, stride=PITCH), :].astype(jnp.bfloat16)
                for e in entries
            ]
            for i, x in enumerate(xs):
                left[pl.ds(o * 16, 16), pl.ds(i * LANES, LANES)] = x
        every = lax.dot_general(
            left[...], fan[...], (((1,), (1,)), ((), ())), preferred_element_type=jnp.float32
        )
        sums = jnp.zeros((16, WIDE), jnp.float32)
        for o in range(PIECE):
            sums = jnp.where(eighth == o, every[o * 16 : o * 16 + 16], sums)
        for h in range(2):
            slots = swap_blocks(sums[:, h * LANES : (h + 1) * LANES])
            names = neuron[pl.ds(2 * b + h, 1), :].astype(jnp.float32)
            names = swap_blocks(jnp.broadcast_to(names, (16, LANES)))
            for g in range(4):
                owner = lax.div(neuron_s[2 * b + h, g * CAP], 768)
                other = across(owner)
                other = jnp.where((other < 0) | (other >= devices), owner, other)
                for to, half in ((owner, 0), (other, 1)):
                    out_ref[pl.ds(to * SLOT + 4 * half, 4), :] = slots[4 * g : 4 * g + 4]
                    at = pl.ds(half * 64, 64)
                    out_ref[pl.ds(to * SLOT + 8, 1), at] = names[4 * g : 4 * g + 1, half * 64 : half * 64 + 64]


def open_kernel(out_ref):
    out_ref[...] = jnp.zeros_like(out_ref)


def opening():
    return pl.pallas_call(
        open_kernel,
        out_shape=jax.ShapeDtypeStruct((8, LANES), jnp.float32),
        out_specs=VMEM,
        compiler_params=pltpu.CompilerParams(vmem_limit_bytes=1 << 20, has_side_effects=True),
        cost_estimate=pl.CostEstimate(flops=10**10, bytes_accessed=10**7, transcendentals=0),
    )()


def contributions(movie, entry_tile, entry_neuron, entry_weights, devices):
    tiles = movie.shape[0]
    entries = entry_tile.shape[0]
    table = (entries // LANES, LANES)
    return pl.pallas_call(
        contrib_kernel,
        out_shape=jax.ShapeDtypeStruct((devices * SLOT, LANES), jnp.float32),
        in_specs=[VMEM] + [HBM] * 3,
        out_specs=VMEM,
        scratch_shapes=[
            pltpu.VMEM((tiles * 2 * PITCH + 16, LANES), jnp.float32),
            pltpu.VMEM((PIECE * 16, PARTS * LANES), jnp.bfloat16),
            pltpu.VMEM((WIDE, PARTS * LANES), jnp.bfloat16),
            pltpu.VMEM((entries, LANES), jnp.bfloat16),
            pltpu.VMEM(table, jnp.int32),
            pltpu.VMEM(table, jnp.int32),
            pltpu.VMEM(table, jnp.int32),
            pltpu.SMEM(table, jnp.int32),
            pltpu.SMEM(table, jnp.int32),
            pltpu.SemaphoreType.DMA((6,)),
        ],
        compiler_params=pltpu.CompilerParams(vmem_limit_bytes=48 << 20),
        cost_estimate=pl.CostEstimate(flops=10**10, bytes_accessed=10**7, transcendentals=0),
    )(movie, entry_tile.reshape(table), entry_neuron.reshape(table), entry_weights)


def gathered(half, block, got_ref, out_ref):
    sources = got_ref.shape[0] // SLOT
    lane = lax.broadcasted_iota(jnp.int32, (1, LANES), 1)
    sub = lax.broadcasted_iota(jnp.int32, (256, LANES), 0).astype(jnp.float32)
    sums = jnp.zeros((96, 256), jnp.float32)
    for b in range(sources // 8):
        lefts, hots = [], []
        for i in range(2):
            row = (2 * b + i) * 4 * SLOT
            r0, r1, r2, r3 = (got_ref[row + s * SLOT + 8 : row + s * SLOT + 9, :] for s in range(4))
            pairs = [jnp.where(lane % 64 < 32, r0, r1), jnp.where(lane % 64 < 32, r2, r3)]
            pairs[1 - half] = pltpu.roll(pairs[1 - half], 64, 1)
            name = jnp.where(lane < 64, *pairs) - (block * 768).astype(jnp.float32)
            x = jnp.concatenate(
                [got_ref[row + s * SLOT + 4 * half : row + s * SLOT + 4 * half + 4, :] for s in range(4)], axis=0
            )
            x = swap_blocks(x)
            high = jnp.where(name >= 512.0, 2.0, jnp.where(name >= 256.0, 1.0, 0.0))
            low = name - 256.0 * high
            big = x.astype(jnp.bfloat16).astype(jnp.float32)
            both = jnp.concatenate([big, x - big], axis=0)
            lefts.append(
                jnp.concatenate([jnp.where(high == float(h), both, 0.0) for h in range(3)], axis=0).astype(jnp.bfloat16)
            )
            hots.append(jnp.where(sub == low, 1.0, 0.0).astype(jnp.bfloat16))
        sums = sums + lax.dot_general(
            jnp.concatenate(lefts, axis=1), jnp.concatenate(hots, axis=1), (((1,), (1,)), ((), ())),
            preferred_element_type=jnp.float32,
        )
    for h in range(3):
        out_ref[:, h * 256 : h * 256 + 256] = sums[h * 32 : h * 32 + 16] + sums[h * 32 + 16 : h * 32 + 32]


def first_kernel(got_ref, ready_ref, out_ref, first_ref):
    gathered(0, place(), got_ref, out_ref)
    first_ref[...] = update(ready_ref[0:16, :], ready_ref[16:32, :], out_ref[...], ready_ref[32:33, :])


def beyond_kernel(got_ref, own_ref, out_ref):
    gathered(1, across(place()), got_ref, out_ref)


def combine(kernel, got, other, outs):
    out = jax.ShapeDtypeStruct((16, other.shape[1]), jnp.float32)
    return pl.pallas_call(
        kernel,
        out_shape=(out,) * outs,
        in_specs=[VMEM] * 2,
        out_specs=(VMEM,) * outs,
        compiler_params=pltpu.CompilerParams(vmem_limit_bytes=16 << 20),
        cost_estimate=pl.CostEstimate(flops=10**10 if outs > 1 else 10**8, bytes_accessed=10**6, transcendentals=0),
    )(got, other)


def halves(x):
    big = x.astype(jnp.bfloat16)
    return big, (x - big.astype(jnp.float32)).astype(jnp.bfloat16)


def times(c, high, low):
    big, rest = halves(c)
    main = jnp.dot(jnp.concatenate([big, rest], 0), high, preferred_element_type=jnp.float32)
    minor = jnp.dot(big, low, preferred_element_type=jnp.float32)
    return (minor + main[16:]) + main[:16]


def prepare_kernel(
    c_hbm, a_ref, b_ref, self_hbm, prev_hbm, next_hbm, out_ref, high_ref, low_ref, near_hbm, c, own, close, far, sem
):
    even = place() % 2 == 0

    def fetch(source, target, i):
        return pltpu.make_async_copy(source, target, sem.at[i])

    def fetch_both(close_hbm, far_hbm):
        fetch(close_hbm, close, 2).start()
        fetch(far_hbm, far, 3).start()

    fetch(c_hbm, c, 0).start()
    fetch(self_hbm, own, 1).start()
    pl.when(even)(lambda: fetch_both(next_hbm, prev_hbm))
    pl.when(jnp.logical_not(even))(lambda: fetch_both(prev_hbm, next_hbm))
    fetch(c_hbm, c, 0).wait()
    fetch(self_hbm, own, 1).wait()
    eye = lax.broadcasted_iota(jnp.int32, (LANES, LANES), 0) == lax.broadcasted_iota(jnp.int32, (LANES, LANES), 1)
    for i in range(own.shape[0] // LANES):
        at = pl.ds(i * LANES, LANES)
        diag = jnp.sum(jnp.where(eye, own[at, at], 0.0), axis=0, keepdims=True)
        out_ref[32:40, at] = jnp.broadcast_to(diag, (8, LANES))
    out_ref[16:32, :] = c[...]
    total = times(c[...], *halves(own[...]))
    fetch(next_hbm, close, 2).wait()
    keep = fetch(close, near_hbm, 4)
    keep.start()
    total = total + times(a_ref[...], *halves(close[...]))
    fetch(prev_hbm, far, 3).wait()
    high_ref[...], low_ref[...] = halves(far[...])
    out_ref[0:16, :] = total + times(b_ref[...], high_ref[...], low_ref[...])
    keep.wait()


def prepare(c, a, b, matrices):
    n = c.shape[1]
    half = jax.ShapeDtypeStruct((n, n), jnp.bfloat16)
    return pl.pallas_call(
        prepare_kernel,
        out_shape=(jax.ShapeDtypeStruct((40, n), jnp.float32), half, half, jax.ShapeDtypeStruct((n, n), jnp.float32)),
        in_specs=[HBM, VMEM, VMEM, HBM, HBM, HBM],
        out_specs=(VMEM,) * 3 + (HBM,),
        scratch_shapes=[pltpu.VMEM(c.shape, jnp.float32)]
        + [pltpu.VMEM((n, n), jnp.float32)] * 3
        + [pltpu.SemaphoreType.DMA((5,))],
        compiler_params=pltpu.CompilerParams(vmem_limit_bytes=PREPARE_MB << 20),
        cost_estimate=pl.CostEstimate(flops=2 * 10**10, bytes_accessed=10**7, transcendentals=0),
    )(c, a, b, *matrices)


def near_kernel(c_ref, a_ref, self_ref, close_ref, out_ref):
    out_ref[...] = times(c_ref[...], *halves(self_ref[...])) + times(a_ref[...], *halves(close_ref[...]))


def near(c, a, own, close):
    return pl.pallas_call(
        near_kernel,
        out_shape=jax.ShapeDtypeStruct(c.shape, jnp.float32),
        in_specs=[VMEM] * 4,
        out_specs=VMEM,
        compiler_params=pltpu.CompilerParams(vmem_limit_bytes=16 << 20),
        cost_estimate=pl.CostEstimate(flops=5 * 10**8, bytes_accessed=10**6, transcendentals=0),
    )(c, a, own, close)


def step_kernel(part_ref, b_ref, high_ref, low_ref, c_ref, projected_ref, ready_ref, out_ref):
    far = times(b_ref[...], high_ref[...], low_ref[...])
    out_ref[...] = update(part_ref[...] + far, c_ref[...], projected_ref[...], ready_ref[32:33, :])


def second_step_kernel(
    last, part_ref, other_ref, beyond_ref, high_ref, low_ref, c_ref, projected_ref, ready_ref, out_ref
):
    block = across(place())
    b = update(other_ref[0:16, :], other_ref[16:32, :], beyond_ref[...], other_ref[32:33, :])
    row = lax.broadcasted_iota(jnp.int32, b.shape, 0)
    b = jnp.where(row < jnp.where((block < 0) | (block > last), 0, 16), b, 0.0)
    far = times(b, high_ref[...], low_ref[...])
    out_ref[...] = update(part_ref[...] + far, c_ref[...], projected_ref[...], ready_ref[32:33, :])


def step(kernel, *operands):
    return pl.pallas_call(
        kernel,
        out_shape=jax.ShapeDtypeStruct(operands[0].shape, jnp.float32),
        in_specs=[VMEM] * len(operands),
        out_specs=VMEM,
        compiler_params=pltpu.CompilerParams(vmem_limit_bytes=16 << 20),
        cost_estimate=pl.CostEstimate(flops=3 * 10**8, bytes_accessed=10**6, transcendentals=0),
    )(*operands)


def swap_in_chip(c):
    n = lax.axis_size(AXES)
    return lax.ppermute(c, AXES, [(i, i ^ 1) for i in range(n)])


def swap_across(c):
    n = lax.axis_size(AXES)
    return lax.ppermute(c, AXES, [(i, across(i)) for i in range(1, n - 1)])


def local(
    movie,
    entry_tile,
    entry_neuron,
    entry_weights,
    intersection_self,
    intersection_prev,
    intersection_next,
    prev_traces,
):
    devices = lax.axis_size(AXES)
    matrices = (intersection_self, intersection_prev, intersection_next)
    c, _ = lax.optimization_barrier((prev_traces, opening()))
    a, b = swap_in_chip(c), swap_across(c)
    here = pltpu.with_memory_space_constraint(movie, pltpu.VMEM)
    send = contributions(here, entry_tile, entry_neuron, entry_weights, devices)
    got = lax.all_to_all(send.reshape(devices, 1, SLOT * LANES), AXES, 0, 0)
    ready, *split, close = prepare(c, a, b, matrices)
    other = swap_across(ready)
    got = got.reshape(devices * SLOT, LANES)
    projected, c = combine(first_kernel, got, ready, 2)
    a = swap_in_chip(c)
    beyond, = combine(beyond_kernel, got, projected, 1)
    part = near(c, a, intersection_self, close)
    second_step = functools.partial(second_step_kernel, devices - 1)
    c = step(second_step, part, other, beyond, *split, c, projected, ready)
    for _ in range(SWEEPS - 2):
        a, b = swap_in_chip(c), swap_across(c)
        part = near(c, a, intersection_self, close)
        c = step(step_kernel, part, b, *split, c, projected, ready)
    return c


def solution(mesh):
    return jax.shard_map(
        local,
        mesh=mesh,
        in_specs=(
            P(AXES, None),
            P(AXES),
            P(AXES),
            P(AXES, None),
            P(AXES, None),
            P(AXES, None),
            P(AXES, None),
            P(None, AXES),
        ),
        out_specs=P(None, AXES),
        check_vma=False,
    )
```

```python
import functools

import jax
import jax.numpy as jnp
from jax import lax
from jax.experimental import pallas as pl
from jax.experimental.pallas import tpu as pltpu
from jax.sharding import PartitionSpec as P

SWEEPS = 3
AXES = ("planes", "rows")
LANES = 128
CAP = 32
SLOT = 9
PREPARE_MB = 50
PITCH = 9
WIDE = 256
PARTS = 8
PIECE = WIDE // PARTS
HBM = pl.BlockSpec(memory_space=pltpu.HBM)
VMEM = pl.BlockSpec(memory_space=pltpu.VMEM)


def place():
    return lax.axis_index(AXES)


def across(block):
    return block + 2 * (block & 1) - 1


def update(coupled, c, projected, diag):
    return jnp.maximum(c + (projected - coupled) / diag, 0.0)


def swap_blocks(x):
    row = lax.broadcasted_iota(jnp.int32, x.shape, 0) // 4
    col = lax.broadcasted_iota(jnp.int32, x.shape, 1) // CAP
    out = x
    for d in range(1, 4):
        moved = pltpu.roll(pltpu.roll(x, CAP * d, 1), 16 - 4 * d, 0)
        out = jnp.where((col - row) % 4 == d, moved, out)
    return out


def contrib_kernel(
    movie_ref, tile_hbm, neuron_hbm, weight_hbm,
    out_ref,
    slab, left, fan, weight, tile, neuron, row, row_s, neuron_s, sem2,
):
    group = 16 * PITCH
    devices = out_ref.shape[0] // SLOT
    small = [
        pltpu.make_async_copy(source, target, sem2.at[i])
        for i, (source, target) in enumerate(
            [
                (tile_hbm, tile),
                (neuron_hbm, neuron),
                (neuron_hbm, neuron_s),
                (weight_hbm, weight),
            ]
        )
    ]
    for copy in small:
        copy.start()
    out_ref[...] = jnp.zeros_like(out_ref)

    def spread(first, last):
        @pl.loop(first, last, unroll=2)
        def _(r):
            base = r * 2 * group
            for f in range(16):
                x = movie_ref[pl.ds(pl.multiple_of(r * 16, 16), 16), pl.ds(f * LANES, LANES)].astype(jnp.float32)
                slab[pl.ds(base + f * PITCH, 8), :] = x[:8]
                slab[pl.ds(base + group + f * PITCH, 8), :] = x[8:]

    steps = movie_ref.shape[0] // 16
    spread(0, steps // 2)
    small[0].wait()
    row[...] = (tile[...] >> 3) * group + (tile[...] & 7)
    to_scalar = pltpu.make_async_copy(row, row_s, sem2.at[5])
    to_scalar.start()
    spread(steps // 2, steps)
    for copy in small[1:]:
        copy.wait()
    to_scalar.wait()
    fan[...] = jnp.zeros_like(fan)
    eighth = lax.broadcasted_iota(jnp.int32, (16, WIDE), 1) % PIECE

    @pl.loop(0, tile.shape[0] * LANES // WIDE, unroll=tile.shape[0] * LANES // WIDE)
    def _(b):
        start = pl.multiple_of(b * WIDE, WIDE)
        for i in range(PARTS):
            fan[pl.ds(PIECE * i, PIECE), pl.ds(i * LANES, LANES)] = weight[pl.ds(start + PIECE * i, PIECE), :]
        for o in range(PIECE):
            entries = [PIECE * i + o for i in range(PARTS)]
            xs = [
                slab[pl.ds(row_s[2 * b + e // LANES, e % LANES], 16, stride=PITCH), :].astype(jnp.bfloat16)
                for e in entries
            ]
            for i, x in enumerate(xs):
                left[pl.ds(o * 16, 16), pl.ds(i * LANES, LANES)] = x
        every = lax.dot_general(
            left[...], fan[...], (((1,), (1,)), ((), ())), preferred_element_type=jnp.float32
        )
        sums = jnp.zeros((16, WIDE), jnp.float32)
        for o in range(PIECE):
            sums = jnp.where(eighth == o, every[o * 16 : o * 16 + 16], sums)
        for h in range(2):
            slots = swap_blocks(sums[:, h * LANES : (h + 1) * LANES])
            names = neuron[pl.ds(2 * b + h, 1), :].astype(jnp.float32)
            names = swap_blocks(jnp.broadcast_to(names, (16, LANES)))
            for g in range(4):
                owner = lax.div(neuron_s[2 * b + h, g * CAP], 768)
                other = across(owner)
                other = jnp.where((other < 0) | (other >= devices), owner, other)
                for to, half in ((owner, 0), (other, 1)):
                    out_ref[pl.ds(to * SLOT + 4 * half, 4), :] = slots[4 * g : 4 * g + 4]
                    at = pl.ds(half * 64, 64)
                    out_ref[pl.ds(to * SLOT + 8, 1), at] = names[4 * g : 4 * g + 1, half * 64 : half * 64 + 64]


def open_kernel(out_ref):
    out_ref[...] = jnp.zeros_like(out_ref)


def opening():
    return pl.pallas_call(
        open_kernel,
        out_shape=jax.ShapeDtypeStruct((8, LANES), jnp.float32),
        out_specs=VMEM,
        compiler_params=pltpu.CompilerParams(vmem_limit_bytes=1 << 20, has_side_effects=True),
        cost_estimate=pl.CostEstimate(flops=10**10, bytes_accessed=10**7, transcendentals=0),
    )()


def contributions(movie, entry_tile, entry_neuron, entry_weights, devices):
    tiles = movie.shape[0]
    entries = entry_tile.shape[0]
    table = (entries // LANES, LANES)
    return pl.pallas_call(
        contrib_kernel,
        out_shape=jax.ShapeDtypeStruct((devices * SLOT, LANES), jnp.float32),
        in_specs=[VMEM] + [HBM] * 3,
        out_specs=VMEM,
        scratch_shapes=[
            pltpu.VMEM((tiles * 2 * PITCH + 16, LANES), jnp.float32),
            pltpu.VMEM((PIECE * 16, PARTS * LANES), jnp.bfloat16),
            pltpu.VMEM((WIDE, PARTS * LANES), jnp.bfloat16),
            pltpu.VMEM((entries, LANES), jnp.bfloat16),
            pltpu.VMEM(table, jnp.int32),
            pltpu.VMEM(table, jnp.int32),
            pltpu.VMEM(table, jnp.int32),
            pltpu.SMEM(table, jnp.int32),
            pltpu.SMEM(table, jnp.int32),
            pltpu.SemaphoreType.DMA((6,)),
        ],
        compiler_params=pltpu.CompilerParams(vmem_limit_bytes=48 << 20),
        cost_estimate=pl.CostEstimate(flops=10**10, bytes_accessed=10**7, transcendentals=0),
    )(movie, entry_tile.reshape(table), entry_neuron.reshape(table), entry_weights)


def gathered(half, block, got_ref, out_ref):
    sources = got_ref.shape[0] // SLOT
    lane = lax.broadcasted_iota(jnp.int32, (1, LANES), 1)
    sub = lax.broadcasted_iota(jnp.int32, (256, LANES), 0).astype(jnp.float32)
    sums = jnp.zeros((96, 256), jnp.float32)
    for b in range(sources // 8):
        lefts, hots = [], []
        for i in range(2):
            row = (2 * b + i) * 4 * SLOT
            r0, r1, r2, r3 = (got_ref[row + s * SLOT + 8 : row + s * SLOT + 9, :] for s in range(4))
            pairs = [jnp.where(lane % 64 < 32, r0, r1), jnp.where(lane % 64 < 32, r2, r3)]
            pairs[1 - half] = pltpu.roll(pairs[1 - half], 64, 1)
            name = jnp.where(lane < 64, *pairs) - (block * 768).astype(jnp.float32)
            x = jnp.concatenate(
                [got_ref[row + s * SLOT + 4 * half : row + s * SLOT + 4 * half + 4, :] for s in range(4)], axis=0
            )
            x = swap_blocks(x)
            high = jnp.where(name >= 512.0, 2.0, jnp.where(name >= 256.0, 1.0, 0.0))
            low = name - 256.0 * high
            big = x.astype(jnp.bfloat16).astype(jnp.float32)
            both = jnp.concatenate([big, x - big], axis=0)
            lefts.append(
                jnp.concatenate([jnp.where(high == float(h), both, 0.0) for h in range(3)], axis=0).astype(jnp.bfloat16)
            )
            hots.append(jnp.where(sub == low, 1.0, 0.0).astype(jnp.bfloat16))
        sums = sums + lax.dot_general(
            jnp.concatenate(lefts, axis=1), jnp.concatenate(hots, axis=1), (((1,), (1,)), ((), ())),
            preferred_element_type=jnp.float32,
        )
    for h in range(3):
        out_ref[:, h * 256 : h * 256 + 256] = sums[h * 32 : h * 32 + 16] + sums[h * 32 + 16 : h * 32 + 32]


def first_kernel(got_ref, ready_ref, out_ref, first_ref):
    gathered(0, place(), got_ref, out_ref)
    first_ref[...] = update(ready_ref[0:16, :], ready_ref[16:32, :], out_ref[...], ready_ref[32:33, :])


def beyond_kernel(got_ref, own_ref, out_ref):
    gathered(1, across(place()), got_ref, out_ref)


def combine(kernel, got, other, outs):
    out = jax.ShapeDtypeStruct((16, other.shape[1]), jnp.float32)
    return pl.pallas_call(
        kernel,
        out_shape=(out,) * outs,
        in_specs=[VMEM] * 2,
        out_specs=(VMEM,) * outs,
        compiler_params=pltpu.CompilerParams(vmem_limit_bytes=16 << 20),
        cost_estimate=pl.CostEstimate(flops=10**10 if outs > 1 else 10**8, bytes_accessed=10**6, transcendentals=0),
    )(got, other)


def halves(x):
    big = x.astype(jnp.bfloat16)
    return big, (x - big.astype(jnp.float32)).astype(jnp.bfloat16)


def times(c, high, low):
    big, rest = halves(c)
    main = jnp.dot(jnp.concatenate([big, rest], 0), high, preferred_element_type=jnp.float32)
    minor = jnp.dot(big, low, preferred_element_type=jnp.float32)
    return (minor + main[16:]) + main[:16]


def prepare_kernel(
    c_hbm, a_ref, b_ref, self_hbm, prev_hbm, next_hbm, out_ref, high_ref, low_ref, near_hbm, c, own, close, far, sem
):
    even = place() % 2 == 0

    def fetch(source, target, i):
        return pltpu.make_async_copy(source, target, sem.at[i])

    def fetch_both(close_hbm, far_hbm):
        fetch(close_hbm, close, 2).start()
        fetch(far_hbm, far, 3).start()

    fetch(c_hbm, c, 0).start()
    fetch(self_hbm, own, 1).start()
    pl.when(even)(lambda: fetch_both(next_hbm, prev_hbm))
    pl.when(jnp.logical_not(even))(lambda: fetch_both(prev_hbm, next_hbm))
    fetch(c_hbm, c, 0).wait()
    fetch(self_hbm, own, 1).wait()
    eye = lax.broadcasted_iota(jnp.int32, (LANES, LANES), 0) == lax.broadcasted_iota(jnp.int32, (LANES, LANES), 1)
    for i in range(own.shape[0] // LANES):
        at = pl.ds(i * LANES, LANES)
        diag = jnp.sum(jnp.where(eye, own[at, at], 0.0), axis=0, keepdims=True)
        out_ref[32:40, at] = jnp.broadcast_to(diag, (8, LANES))
    out_ref[16:32, :] = c[...]
    total = times(c[...], *halves(own[...]))
    fetch(next_hbm, close, 2).wait()
    keep = fetch(close, near_hbm, 4)
    keep.start()
    total = total + times(a_ref[...], *halves(close[...]))
    fetch(prev_hbm, far, 3).wait()
    high_ref[...], low_ref[...] = halves(far[...])
    out_ref[0:16, :] = total + times(b_ref[...], high_ref[...], low_ref[...])
    keep.wait()


def prepare(c, a, b, matrices):
    n = c.shape[1]
    half = jax.ShapeDtypeStruct((n, n), jnp.bfloat16)
    return pl.pallas_call(
        prepare_kernel,
        out_shape=(jax.ShapeDtypeStruct((40, n), jnp.float32), half, half, jax.ShapeDtypeStruct((n, n), jnp.float32)),
        in_specs=[HBM, VMEM, VMEM, HBM, HBM, HBM],
        out_specs=(VMEM,) * 3 + (HBM,),
        scratch_shapes=[pltpu.VMEM(c.shape, jnp.float32)]
        + [pltpu.VMEM((n, n), jnp.float32)] * 3
        + [pltpu.SemaphoreType.DMA((5,))],
        compiler_params=pltpu.CompilerParams(vmem_limit_bytes=PREPARE_MB << 20),
        cost_estimate=pl.CostEstimate(flops=2 * 10**10, bytes_accessed=10**7, transcendentals=0),
    )(c, a, b, *matrices)


def near_kernel(c_ref, a_ref, self_ref, close_ref, out_ref):
    out_ref[...] = times(c_ref[...], *halves(self_ref[...])) + times(a_ref[...], *halves(close_ref[...]))


def near(c, a, own, close):
    return pl.pallas_call(
        near_kernel,
        out_shape=jax.ShapeDtypeStruct(c.shape, jnp.float32),
        in_specs=[VMEM] * 4,
        out_specs=VMEM,
        compiler_params=pltpu.CompilerParams(vmem_limit_bytes=16 << 20),
        cost_estimate=pl.CostEstimate(flops=5 * 10**8, bytes_accessed=10**6, transcendentals=0),
    )(c, a, own, close)


def step_kernel(part_ref, b_ref, high_ref, low_ref, c_ref, projected_ref, ready_ref, out_ref):
    far = times(b_ref[...], high_ref[...], low_ref[...])
    out_ref[...] = update(part_ref[...] + far, c_ref[...], projected_ref[...], ready_ref[32:33, :])


def second_step_kernel(
    last, part_ref, other_ref, beyond_ref, high_ref, low_ref, c_ref, projected_ref, ready_ref, out_ref
):
    block = across(place())
    b = update(other_ref[0:16, :], other_ref[16:32, :], beyond_ref[...], other_ref[32:33, :])
    row = lax.broadcasted_iota(jnp.int32, b.shape, 0)
    b = jnp.where(row < jnp.where((block < 0) | (block > last), 0, 16), b, 0.0)
    far = times(b, high_ref[...], low_ref[...])
    out_ref[...] = update(part_ref[...] + far, c_ref[...], projected_ref[...], ready_ref[32:33, :])


def step(kernel, *operands):
    return pl.pallas_call(
        kernel,
        out_shape=jax.ShapeDtypeStruct(operands[0].shape, jnp.float32),
        in_specs=[VMEM] * len(operands),
        out_specs=VMEM,
        compiler_params=pltpu.CompilerParams(vmem_limit_bytes=16 << 20),
        cost_estimate=pl.CostEstimate(flops=3 * 10**8, bytes_accessed=10**6, transcendentals=0),
    )(*operands)


def swap_in_chip(c):
    n = lax.axis_size(AXES)
    return lax.ppermute(c, AXES, [(i, i ^ 1) for i in range(n)])


def swap_across(c):
    n = lax.axis_size(AXES)
    return lax.ppermute(c, AXES, [(i, across(i)) for i in range(1, n - 1)])


def local(
    movie,
    entry_tile,
    entry_neuron,
    entry_weights,
    intersection_self,
    intersection_prev,
    intersection_next,
    prev_traces,
):
    devices = lax.axis_size(AXES)
    matrices = (intersection_self, intersection_prev, intersection_next)
    c, _ = lax.optimization_barrier((prev_traces, opening()))
    a, b = swap_in_chip(c), swap_across(c)
    here = pltpu.with_memory_space_constraint(movie, pltpu.VMEM)
    send = contributions(here, entry_tile, entry_neuron, entry_weights, devices)
    got = lax.all_to_all(send.reshape(devices, 1, SLOT * LANES), AXES, 0, 0)
    ready, *split, close = prepare(c, a, b, matrices)
    other = swap_across(ready)
    got = got.reshape(devices * SLOT, LANES)
    projected, c = combine(first_kernel, got, ready, 2)
    a = swap_in_chip(c)
    beyond, = combine(beyond_kernel, got, projected, 1)
    part = near(c, a, intersection_self, close)
    second_step = functools.partial(second_step_kernel, devices - 1)
    c = step(second_step, part, other, beyond, *split, c, projected, ready)
    for _ in range(SWEEPS - 2):
        a, b = swap_in_chip(c), swap_across(c)
        part = near(c, a, intersection_self, close)
        c = step(step_kernel, part, b, *split, c, projected, ready)
    return c


def solution(mesh):
    return jax.shard_map(
        local,
        mesh=mesh,
        in_specs=(
            P(AXES, None),
            P(AXES),
            P(AXES),
            P(AXES, None),
            P(AXES, None),
            P(AXES, None),
            P(AXES, None),
            P(None, AXES),
        ),
        out_specs=P(None, AXES),
        check_vma=False,
    )
```

```python
import functools

import jax
import jax.numpy as jnp
from jax import lax
from jax.experimental import pallas as pl
from jax.experimental.pallas import tpu as pltpu
from jax.sharding import PartitionSpec as P

SWEEPS = 3
AXES = ("planes", "rows")
LANES = 128
CAP = 32
SLOT = 9
PREPARE_MB = 50
PITCH = 9
WIDE = 256
PARTS = 8
PIECE = WIDE // PARTS
HBM = pl.BlockSpec(memory_space=pltpu.HBM)
VMEM = pl.BlockSpec(memory_space=pltpu.VMEM)


def place():
    return lax.axis_index(AXES)


def across(block):
    return block + 2 * (block & 1) - 1


def update(coupled, c, projected, diag):
    return jnp.maximum(c + (projected - coupled) / diag, 0.0)


def swap_blocks(x):
    row = lax.broadcasted_iota(jnp.int32, x.shape, 0) // 4
    col = lax.broadcasted_iota(jnp.int32, x.shape, 1) // CAP
    out = x
    for d in range(1, 4):
        moved = pltpu.roll(pltpu.roll(x, CAP * d, 1), 16 - 4 * d, 0)
        out = jnp.where((col - row) % 4 == d, moved, out)
    return out


def contrib_kernel(
    movie_ref, tile_hbm, neuron_hbm, weight_hbm,
    out_ref,
    slab, left, fan, weight, tile, neuron, row, row_s, neuron_s, sem2,
):
    group = 16 * PITCH
    devices = out_ref.shape[0] // SLOT
    small = [
        pltpu.make_async_copy(source, target, sem2.at[i])
        for i, (source, target) in enumerate(
            [
                (tile_hbm, tile),
                (neuron_hbm, neuron),
                (neuron_hbm, neuron_s),
                (weight_hbm, weight),
            ]
        )
    ]
    for copy in small:
        copy.start()
    out_ref[...] = jnp.zeros_like(out_ref)

    def spread(first, last):
        @pl.loop(first, last, unroll=4)
        def _(r):
            base = r * 2 * group
            for f in range(16):
                x = movie_ref[pl.ds(pl.multiple_of(r * 16, 16), 16), pl.ds(f * LANES, LANES)].astype(jnp.float32)
                slab[pl.ds(base + f * PITCH, 8), :] = x[:8]
                slab[pl.ds(base + group + f * PITCH, 8), :] = x[8:]

    steps = movie_ref.shape[0] // 16
    spread(0, steps // 2)
    small[0].wait()
    row[...] = (tile[...] >> 3) * group + (tile[...] & 7)
    to_scalar = pltpu.make_async_copy(row, row_s, sem2.at[5])
    to_scalar.start()
    spread(steps // 2, steps)
    for copy in small[1:]:
        copy.wait()
    to_scalar.wait()
    fan[...] = jnp.zeros_like(fan)
    eighth = lax.broadcasted_iota(jnp.int32, (16, WIDE), 1) % PIECE

    @pl.loop(0, tile.shape[0] * LANES // WIDE, unroll=tile.shape[0] * LANES // WIDE)
    def _(b):
        start = pl.multiple_of(b * WIDE, WIDE)
        for i in range(PARTS):
            fan[pl.ds(PIECE * i, PIECE), pl.ds(i * LANES, LANES)] = weight[pl.ds(start + PIECE * i, PIECE), :]
        for o in range(PIECE):
            entries = [PIECE * i + o for i in range(PARTS)]
            xs = [
                slab[pl.ds(row_s[2 * b + e // LANES, e % LANES], 16, stride=PITCH), :].astype(jnp.bfloat16)
                for e in entries
            ]
            for i, x in enumerate(xs):
                left[pl.ds(o * 16, 16), pl.ds(i * LANES, LANES)] = x
        every = lax.dot_general(
            left[...], fan[...], (((1,), (1,)), ((), ())), preferred_element_type=jnp.float32
        )
        sums = jnp.zeros((16, WIDE), jnp.float32)
        for o in range(PIECE):
            sums = jnp.where(eighth == o, every[o * 16 : o * 16 + 16], sums)
        for h in range(2):
            slots = swap_blocks(sums[:, h * LANES : (h + 1) * LANES])
            names = neuron[pl.ds(2 * b + h, 1), :].astype(jnp.float32)
            names = swap_blocks(jnp.broadcast_to(names, (16, LANES)))
            for g in range(4):
                owner = lax.div(neuron_s[2 * b + h, g * CAP], 768)
                other = across(owner)
                other = jnp.where((other < 0) | (other >= devices), owner, other)
                for to, half in ((owner, 0), (other, 1)):
                    out_ref[pl.ds(to * SLOT + 4 * half, 4), :] = slots[4 * g : 4 * g + 4]
                    at = pl.ds(half * 64, 64)
                    out_ref[pl.ds(to * SLOT + 8, 1), at] = names[4 * g : 4 * g + 1, half * 64 : half * 64 + 64]


def open_kernel(out_ref):
    out_ref[...] = jnp.zeros_like(out_ref)


def opening():
    return pl.pallas_call(
        open_kernel,
        out_shape=jax.ShapeDtypeStruct((8, LANES), jnp.float32),
        out_specs=VMEM,
        compiler_params=pltpu.CompilerParams(vmem_limit_bytes=1 << 20, has_side_effects=True),
        cost_estimate=pl.CostEstimate(flops=10**10, bytes_accessed=10**7, transcendentals=0),
    )()


def contributions(movie, entry_tile, entry_neuron, entry_weights, devices):
    tiles = movie.shape[0]
    entries = entry_tile.shape[0]
    table = (entries // LANES, LANES)
    return pl.pallas_call(
        contrib_kernel,
        out_shape=jax.ShapeDtypeStruct((devices * SLOT, LANES), jnp.float32),
        in_specs=[VMEM] + [HBM] * 3,
        out_specs=VMEM,
        scratch_shapes=[
            pltpu.VMEM((tiles * 2 * PITCH + 16, LANES), jnp.float32),
            pltpu.VMEM((PIECE * 16, PARTS * LANES), jnp.bfloat16),
            pltpu.VMEM((WIDE, PARTS * LANES), jnp.bfloat16),
            pltpu.VMEM((entries, LANES), jnp.bfloat16),
            pltpu.VMEM(table, jnp.int32),
            pltpu.VMEM(table, jnp.int32),
            pltpu.VMEM(table, jnp.int32),
            pltpu.SMEM(table, jnp.int32),
            pltpu.SMEM(table, jnp.int32),
            pltpu.SemaphoreType.DMA((6,)),
        ],
        compiler_params=pltpu.CompilerParams(vmem_limit_bytes=48 << 20),
        cost_estimate=pl.CostEstimate(flops=10**10, bytes_accessed=10**7, transcendentals=0),
    )(movie, entry_tile.reshape(table), entry_neuron.reshape(table), entry_weights)


def gathered(half, block, got_ref, out_ref):
    sources = got_ref.shape[0] // SLOT
    lane = lax.broadcasted_iota(jnp.int32, (1, LANES), 1)
    sub = lax.broadcasted_iota(jnp.int32, (256, LANES), 0).astype(jnp.float32)
    sums = jnp.zeros((96, 256), jnp.float32)
    for b in range(sources // 8):
        lefts, hots = [], []
        for i in range(2):
            row = (2 * b + i) * 4 * SLOT
            r0, r1, r2, r3 = (got_ref[row + s * SLOT + 8 : row + s * SLOT + 9, :] for s in range(4))
            pairs = [jnp.where(lane % 64 < 32, r0, r1), jnp.where(lane % 64 < 32, r2, r3)]
            pairs[1 - half] = pltpu.roll(pairs[1 - half], 64, 1)
            name = jnp.where(lane < 64, *pairs) - (block * 768).astype(jnp.float32)
            x = jnp.concatenate(
                [got_ref[row + s * SLOT + 4 * half : row + s * SLOT + 4 * half + 4, :] for s in range(4)], axis=0
            )
            x = swap_blocks(x)
            high = jnp.where(name >= 512.0, 2.0, jnp.where(name >= 256.0, 1.0, 0.0))
            low = name - 256.0 * high
            big = x.astype(jnp.bfloat16).astype(jnp.float32)
            both = jnp.concatenate([big, x - big], axis=0)
            lefts.append(
                jnp.concatenate([jnp.where(high == float(h), both, 0.0) for h in range(3)], axis=0).astype(jnp.bfloat16)
            )
            hots.append(jnp.where(sub == low, 1.0, 0.0).astype(jnp.bfloat16))
        sums = sums + lax.dot_general(
            jnp.concatenate(lefts, axis=1), jnp.concatenate(hots, axis=1), (((1,), (1,)), ((), ())),
            preferred_element_type=jnp.float32,
        )
    for h in range(3):
        out_ref[:, h * 256 : h * 256 + 256] = sums[h * 32 : h * 32 + 16] + sums[h * 32 + 16 : h * 32 + 32]


def first_kernel(got_ref, ready_ref, out_ref, first_ref):
    gathered(0, place(), got_ref, out_ref)
    first_ref[...] = update(ready_ref[0:16, :], ready_ref[16:32, :], out_ref[...], ready_ref[32:33, :])


def beyond_kernel(got_ref, own_ref, out_ref):
    gathered(1, across(place()), got_ref, out_ref)


def combine(kernel, got, other, outs):
    out = jax.ShapeDtypeStruct((16, other.shape[1]), jnp.float32)
    return pl.pallas_call(
        kernel,
        out_shape=(out,) * outs,
        in_specs=[VMEM] * 2,
        out_specs=(VMEM,) * outs,
        compiler_params=pltpu.CompilerParams(vmem_limit_bytes=16 << 20),
        cost_estimate=pl.CostEstimate(flops=10**10 if outs > 1 else 10**8, bytes_accessed=10**6, transcendentals=0),
    )(got, other)


def halves(x):
    big = x.astype(jnp.bfloat16)
    return big, (x - big.astype(jnp.float32)).astype(jnp.bfloat16)


def times(c, high, low):
    big, rest = halves(c)
    main = jnp.dot(jnp.concatenate([big, rest], 0), high, preferred_element_type=jnp.float32)
    minor = jnp.dot(big, low, preferred_element_type=jnp.float32)
    return (minor + main[16:]) + main[:16]


def prepare_kernel(
    c_hbm, a_ref, b_ref, self_hbm, prev_hbm, next_hbm, out_ref, high_ref, low_ref, near_hbm, c, own, close, far, sem
):
    even = place() % 2 == 0

    def fetch(source, target, i):
        return pltpu.make_async_copy(source, target, sem.at[i])

    def fetch_both(close_hbm, far_hbm):
        fetch(close_hbm, close, 2).start()
        fetch(far_hbm, far, 3).start()

    fetch(c_hbm, c, 0).start()
    fetch(self_hbm, own, 1).start()
    pl.when(even)(lambda: fetch_both(next_hbm, prev_hbm))
    pl.when(jnp.logical_not(even))(lambda: fetch_both(prev_hbm, next_hbm))
    fetch(c_hbm, c, 0).wait()
    fetch(self_hbm, own, 1).wait()
    eye = lax.broadcasted_iota(jnp.int32, (LANES, LANES), 0) == lax.broadcasted_iota(jnp.int32, (LANES, LANES), 1)
    for i in range(own.shape[0] // LANES):
        at = pl.ds(i * LANES, LANES)
        diag = jnp.sum(jnp.where(eye, own[at, at], 0.0), axis=0, keepdims=True)
        out_ref[32:40, at] = jnp.broadcast_to(diag, (8, LANES))
    out_ref[16:32, :] = c[...]
    total = times(c[...], *halves(own[...]))
    fetch(next_hbm, close, 2).wait()
    keep = fetch(close, near_hbm, 4)
    keep.start()
    total = total + times(a_ref[...], *halves(close[...]))
    fetch(prev_hbm, far, 3).wait()
    high_ref[...], low_ref[...] = halves(far[...])
    out_ref[0:16, :] = total + times(b_ref[...], high_ref[...], low_ref[...])
    keep.wait()


def prepare(c, a, b, matrices):
    n = c.shape[1]
    half = jax.ShapeDtypeStruct((n, n), jnp.bfloat16)
    return pl.pallas_call(
        prepare_kernel,
        out_shape=(jax.ShapeDtypeStruct((40, n), jnp.float32), half, half, jax.ShapeDtypeStruct((n, n), jnp.float32)),
        in_specs=[HBM, VMEM, VMEM, HBM, HBM, HBM],
        out_specs=(VMEM,) * 3 + (HBM,),
        scratch_shapes=[pltpu.VMEM(c.shape, jnp.float32)]
        + [pltpu.VMEM((n, n), jnp.float32)] * 3
        + [pltpu.SemaphoreType.DMA((5,))],
        compiler_params=pltpu.CompilerParams(vmem_limit_bytes=PREPARE_MB << 20),
        cost_estimate=pl.CostEstimate(flops=2 * 10**10, bytes_accessed=10**7, transcendentals=0),
    )(c, a, b, *matrices)


def near_kernel(c_ref, a_ref, self_ref, close_ref, out_ref):
    out_ref[...] = times(c_ref[...], *halves(self_ref[...])) + times(a_ref[...], *halves(close_ref[...]))


def near(c, a, own, close):
    return pl.pallas_call(
        near_kernel,
        out_shape=jax.ShapeDtypeStruct(c.shape, jnp.float32),
        in_specs=[VMEM] * 4,
        out_specs=VMEM,
        compiler_params=pltpu.CompilerParams(vmem_limit_bytes=16 << 20),
        cost_estimate=pl.CostEstimate(flops=5 * 10**8, bytes_accessed=10**6, transcendentals=0),
    )(c, a, own, close)


def step_kernel(part_ref, b_ref, high_ref, low_ref, c_ref, projected_ref, ready_ref, out_ref):
    far = times(b_ref[...], high_ref[...], low_ref[...])
    out_ref[...] = update(part_ref[...] + far, c_ref[...], projected_ref[...], ready_ref[32:33, :])


def second_step_kernel(
    last, part_ref, other_ref, beyond_ref, high_ref, low_ref, c_ref, projected_ref, ready_ref, out_ref
):
    block = across(place())
    b = update(other_ref[0:16, :], other_ref[16:32, :], beyond_ref[...], other_ref[32:33, :])
    row = lax.broadcasted_iota(jnp.int32, b.shape, 0)
    b = jnp.where(row < jnp.where((block < 0) | (block > last), 0, 16), b, 0.0)
    far = times(b, high_ref[...], low_ref[...])
    out_ref[...] = update(part_ref[...] + far, c_ref[...], projected_ref[...], ready_ref[32:33, :])


def step(kernel, *operands):
    return pl.pallas_call(
        kernel,
        out_shape=jax.ShapeDtypeStruct(operands[0].shape, jnp.float32),
        in_specs=[VMEM] * len(operands),
        out_specs=VMEM,
        compiler_params=pltpu.CompilerParams(vmem_limit_bytes=16 << 20),
        cost_estimate=pl.CostEstimate(flops=3 * 10**8, bytes_accessed=10**6, transcendentals=0),
    )(*operands)


def swap_in_chip(c):
    n = lax.axis_size(AXES)
    return lax.ppermute(c, AXES, [(i, i ^ 1) for i in range(n)])


def swap_across(c):
    n = lax.axis_size(AXES)
    return lax.ppermute(c, AXES, [(i, across(i)) for i in range(1, n - 1)])


def local(
    movie,
    entry_tile,
    entry_neuron,
    entry_weights,
    intersection_self,
    intersection_prev,
    intersection_next,
    prev_traces,
):
    devices = lax.axis_size(AXES)
    matrices = (intersection_self, intersection_prev, intersection_next)
    c, _ = lax.optimization_barrier((prev_traces, opening()))
    a, b = swap_in_chip(c), swap_across(c)
    here = pltpu.with_memory_space_constraint(movie, pltpu.VMEM)
    send = contributions(here, entry_tile, entry_neuron, entry_weights, devices)
    got = lax.all_to_all(send.reshape(devices, 1, SLOT * LANES), AXES, 0, 0)
    ready, *split, close = prepare(c, a, b, matrices)
    other = swap_across(ready)
    got = got.reshape(devices * SLOT, LANES)
    projected, c = combine(first_kernel, got, ready, 2)
    a = swap_in_chip(c)
    beyond, = combine(beyond_kernel, got, projected, 1)
    part = near(c, a, intersection_self, close)
    second_step = functools.partial(second_step_kernel, devices - 1)
    c = step(second_step, part, other, beyond, *split, c, projected, ready)
    for _ in range(SWEEPS - 2):
        a, b = swap_in_chip(c), swap_across(c)
        part = near(c, a, intersection_self, close)
        c = step(step_kernel, part, b, *split, c, projected, ready)
    return c


def solution(mesh):
    return jax.shard_map(
        local,
        mesh=mesh,
        in_specs=(
            P(AXES, None),
            P(AXES),
            P(AXES),
            P(AXES, None),
            P(AXES, None),
            P(AXES, None),
            P(AXES, None),
            P(None, AXES),
        ),
        out_specs=P(None, AXES),
        check_vma=False,
    )
```

```python
import functools

import jax
import jax.numpy as jnp
from jax import lax
from jax.experimental import pallas as pl
from jax.experimental.pallas import tpu as pltpu
from jax.sharding import PartitionSpec as P

SWEEPS = 3
AXES = ("planes", "rows")
LANES = 128
CAP = 32
SLOT = 9
PREPARE_MB = 50
PITCH = 9
WIDE = 256
PARTS = 8
PIECE = WIDE // PARTS
HBM = pl.BlockSpec(memory_space=pltpu.HBM)
VMEM = pl.BlockSpec(memory_space=pltpu.VMEM)


def place():
    return lax.axis_index(AXES)


def across(block):
    return block + 2 * (block & 1) - 1


def update(coupled, c, projected, diag):
    return jnp.maximum(c + (projected - coupled) / diag, 0.0)


def swap_blocks(x):
    row = lax.broadcasted_iota(jnp.int32, x.shape, 0) // 4
    col = lax.broadcasted_iota(jnp.int32, x.shape, 1) // CAP
    out = x
    for d in range(1, 4):
        moved = pltpu.roll(pltpu.roll(x, CAP * d, 1), 16 - 4 * d, 0)
        out = jnp.where((col - row) % 4 == d, moved, out)
    return out


def contrib_kernel(
    movie_ref, tile_hbm, neuron_hbm, weight_hbm,
    out_ref,
    slab, left, fan, weight, tile, neuron, row, row_s, neuron_s, sem2,
):
    group = 16 * PITCH
    devices = out_ref.shape[0] // SLOT
    small = [
        pltpu.make_async_copy(source, target, sem2.at[i])
        for i, (source, target) in enumerate(
            [
                (tile_hbm, tile),
                (neuron_hbm, neuron),
                (neuron_hbm, neuron_s),
                (weight_hbm, weight),
            ]
        )
    ]
    for copy in small:
        copy.start()
    out_ref[...] = jnp.zeros_like(out_ref)

    def spread(first, last):
        @pl.loop(first, last, unroll=2)
        def _(r):
            base = r * 2 * group
            for f in range(16):
                x = movie_ref[pl.ds(pl.multiple_of(r * 16, 16), 16), pl.ds(f * LANES, LANES)].astype(jnp.float32)
                slab[pl.ds(base + f * PITCH, 8), :] = x[:8]
                slab[pl.ds(base + group + f * PITCH, 8), :] = x[8:]

    steps = movie_ref.shape[0] // 16
    spread(0, steps // 2)
    small[0].wait()
    row[...] = (tile[...] >> 3) * group + (tile[...] & 7)
    to_scalar = pltpu.make_async_copy(row, row_s, sem2.at[5])
    to_scalar.start()
    spread(steps // 2, steps)
    for copy in small[1:]:
        copy.wait()
    to_scalar.wait()
    fan[...] = jnp.zeros_like(fan)
    eighth = lax.broadcasted_iota(jnp.int32, (16, WIDE), 1) % PIECE

    @pl.loop(0, tile.shape[0] * LANES // WIDE, unroll=tile.shape[0] * LANES // WIDE)
    def _(b):
        start = pl.multiple_of(b * WIDE, WIDE)
        for i in range(PARTS):
            fan[pl.ds(PIECE * i, PIECE), pl.ds(i * LANES, LANES)] = weight[pl.ds(start + PIECE * i, PIECE), :]
        for o in range(PIECE):
            entries = [PIECE * i + o for i in range(PARTS)]
            xs = [
                slab[pl.ds(row_s[2 * b + e // LANES, e % LANES], 16, stride=PITCH), :].astype(jnp.bfloat16)
                for e in entries
            ]
            for i, x in enumerate(xs):
                left[pl.ds(o * 16, 16), pl.ds(i * LANES, LANES)] = x
        every = lax.dot_general(
            left[...], fan[...], (((1,), (1,)), ((), ())), preferred_element_type=jnp.float32
        )
        sums = jnp.zeros((16, WIDE), jnp.float32)
        for o in range(PIECE):
            sums = jnp.where(eighth == o, every[o * 16 : o * 16 + 16], sums)
        for h in range(2):
            slots = swap_blocks(sums[:, h * LANES : (h + 1) * LANES])
            names = neuron[pl.ds(2 * b + h, 1), :].astype(jnp.float32)
            names = swap_blocks(jnp.broadcast_to(names, (16, LANES)))
            for g in range(4):
                owner = lax.div(neuron_s[2 * b + h, g * CAP], 768)
                other = across(owner)
                other = jnp.where((other < 0) | (other >= devices), owner, other)
                for to, half in ((owner, 0), (other, 1)):
                    out_ref[pl.ds(to * SLOT + 4 * half, 4), :] = slots[4 * g : 4 * g + 4]
                    at = pl.ds(half * 64, 64)
                    out_ref[pl.ds(to * SLOT + 8, 1), at] = names[4 * g : 4 * g + 1, half * 64 : half * 64 + 64]


def open_kernel(out_ref):
    del out_ref


def opening():
    return pl.pallas_call(
        open_kernel,
        out_shape=jax.ShapeDtypeStruct((8, LANES), jnp.float32),
        out_specs=HBM,
        compiler_params=pltpu.CompilerParams(vmem_limit_bytes=1 << 20, has_side_effects=True),
        cost_estimate=pl.CostEstimate(flops=10**10, bytes_accessed=10**7, transcendentals=0),
    )()


def contributions(movie, entry_tile, entry_neuron, entry_weights, devices):
    tiles = movie.shape[0]
    entries = entry_tile.shape[0]
    table = (entries // LANES, LANES)
    return pl.pallas_call(
        contrib_kernel,
        out_shape=jax.ShapeDtypeStruct((devices * SLOT, LANES), jnp.float32),
        in_specs=[VMEM] + [HBM] * 3,
        out_specs=VMEM,
        scratch_shapes=[
            pltpu.VMEM((tiles * 2 * PITCH + 16, LANES), jnp.float32),
            pltpu.VMEM((PIECE * 16, PARTS * LANES), jnp.bfloat16),
            pltpu.VMEM((WIDE, PARTS * LANES), jnp.bfloat16),
            pltpu.VMEM((entries, LANES), jnp.bfloat16),
            pltpu.VMEM(table, jnp.int32),
            pltpu.VMEM(table, jnp.int32),
            pltpu.VMEM(table, jnp.int32),
            pltpu.SMEM(table, jnp.int32),
            pltpu.SMEM(table, jnp.int32),
            pltpu.SemaphoreType.DMA((6,)),
        ],
        compiler_params=pltpu.CompilerParams(vmem_limit_bytes=48 << 20),
        cost_estimate=pl.CostEstimate(flops=10**10, bytes_accessed=10**7, transcendentals=0),
    )(movie, entry_tile.reshape(table), entry_neuron.reshape(table), entry_weights)


def gathered(half, block, got_ref, out_ref):
    sources = got_ref.shape[0] // SLOT
    lane = lax.broadcasted_iota(jnp.int32, (1, LANES), 1)
    sub = lax.broadcasted_iota(jnp.int32, (256, LANES), 0).astype(jnp.float32)
    sums = jnp.zeros((96, 256), jnp.float32)
    for b in range(sources // 8):
        lefts, hots = [], []
        for i in range(2):
            row = (2 * b + i) * 4 * SLOT
            r0, r1, r2, r3 = (got_ref[row + s * SLOT + 8 : row + s * SLOT + 9, :] for s in range(4))
            pairs = [jnp.where(lane % 64 < 32, r0, r1), jnp.where(lane % 64 < 32, r2, r3)]
            pairs[1 - half] = pltpu.roll(pairs[1 - half], 64, 1)
            name = jnp.where(lane < 64, *pairs) - (block * 768).astype(jnp.float32)
            x = jnp.concatenate(
                [got_ref[row + s * SLOT + 4 * half : row + s * SLOT + 4 * half + 4, :] for s in range(4)], axis=0
            )
            x = swap_blocks(x)
            high = jnp.where(name >= 512.0, 2.0, jnp.where(name >= 256.0, 1.0, 0.0))
            low = name - 256.0 * high
            big = x.astype(jnp.bfloat16).astype(jnp.float32)
            both = jnp.concatenate([big, x - big], axis=0)
            lefts.append(
                jnp.concatenate([jnp.where(high == float(h), both, 0.0) for h in range(3)], axis=0).astype(jnp.bfloat16)
            )
            hots.append(jnp.where(sub == low, 1.0, 0.0).astype(jnp.bfloat16))
        sums = sums + lax.dot_general(
            jnp.concatenate(lefts, axis=1), jnp.concatenate(hots, axis=1), (((1,), (1,)), ((), ())),
            preferred_element_type=jnp.float32,
        )
    for h in range(3):
        out_ref[:, h * 256 : h * 256 + 256] = sums[h * 32 : h * 32 + 16] + sums[h * 32 + 16 : h * 32 + 32]


def first_kernel(got_ref, ready_ref, out_ref, first_ref):
    gathered(0, place(), got_ref, out_ref)
    first_ref[...] = update(ready_ref[0:16, :], ready_ref[16:32, :], out_ref[...], ready_ref[32:33, :])


def beyond_kernel(got_ref, own_ref, out_ref):
    gathered(1, across(place()), got_ref, out_ref)


def combine(kernel, got, other, outs):
    out = jax.ShapeDtypeStruct((16, other.shape[1]), jnp.float32)
    return pl.pallas_call(
        kernel,
        out_shape=(out,) * outs,
        in_specs=[VMEM] * 2,
        out_specs=(VMEM,) * outs,
        compiler_params=pltpu.CompilerParams(vmem_limit_bytes=16 << 20),
        cost_estimate=pl.CostEstimate(flops=10**10 if outs > 1 else 10**8, bytes_accessed=10**6, transcendentals=0),
    )(got, other)


def halves(x):
    big = x.astype(jnp.bfloat16)
    return big, (x - big.astype(jnp.float32)).astype(jnp.bfloat16)


def times(c, high, low):
    big, rest = halves(c)
    main = jnp.dot(jnp.concatenate([big, rest], 0), high, preferred_element_type=jnp.float32)
    minor = jnp.dot(big, low, preferred_element_type=jnp.float32)
    return (minor + main[16:]) + main[:16]


def prepare_kernel(
    c_hbm, a_ref, b_ref, self_hbm, prev_hbm, next_hbm, out_ref, high_ref, low_ref, near_hbm, c, own, close, far, sem
):
    even = place() % 2 == 0

    def fetch(source, target, i):
        return pltpu.make_async_copy(source, target, sem.at[i])

    def fetch_both(close_hbm, far_hbm):
        fetch(close_hbm, close, 2).start()
        fetch(far_hbm, far, 3).start()

    fetch(c_hbm, c, 0).start()
    fetch(self_hbm, own, 1).start()
    pl.when(even)(lambda: fetch_both(next_hbm, prev_hbm))
    pl.when(jnp.logical_not(even))(lambda: fetch_both(prev_hbm, next_hbm))
    fetch(c_hbm, c, 0).wait()
    fetch(self_hbm, own, 1).wait()
    eye = lax.broadcasted_iota(jnp.int32, (LANES, LANES), 0) == lax.broadcasted_iota(jnp.int32, (LANES, LANES), 1)
    for i in range(own.shape[0] // LANES):
        at = pl.ds(i * LANES, LANES)
        diag = jnp.sum(jnp.where(eye, own[at, at], 0.0), axis=0, keepdims=True)
        out_ref[32:40, at] = jnp.broadcast_to(diag, (8, LANES))
    out_ref[16:32, :] = c[...]
    total = times(c[...], *halves(own[...]))
    fetch(next_hbm, close, 2).wait()
    keep = fetch(close, near_hbm, 4)
    keep.start()
    total = total + times(a_ref[...], *halves(close[...]))
    fetch(prev_hbm, far, 3).wait()
    high_ref[...], low_ref[...] = halves(far[...])
    out_ref[0:16, :] = total + times(b_ref[...], high_ref[...], low_ref[...])
    keep.wait()


def prepare(c, a, b, matrices):
    n = c.shape[1]
    half = jax.ShapeDtypeStruct((n, n), jnp.bfloat16)
    return pl.pallas_call(
        prepare_kernel,
        out_shape=(jax.ShapeDtypeStruct((40, n), jnp.float32), half, half, jax.ShapeDtypeStruct((n, n), jnp.float32)),
        in_specs=[HBM, VMEM, VMEM, HBM, HBM, HBM],
        out_specs=(VMEM,) * 3 + (HBM,),
        scratch_shapes=[pltpu.VMEM(c.shape, jnp.float32)]
        + [pltpu.VMEM((n, n), jnp.float32)] * 3
        + [pltpu.SemaphoreType.DMA((5,))],
        compiler_params=pltpu.CompilerParams(vmem_limit_bytes=PREPARE_MB << 20),
        cost_estimate=pl.CostEstimate(flops=2 * 10**10, bytes_accessed=10**7, transcendentals=0),
    )(c, a, b, *matrices)


def near_kernel(c_ref, a_ref, self_ref, close_ref, out_ref):
    out_ref[...] = times(c_ref[...], *halves(self_ref[...])) + times(a_ref[...], *halves(close_ref[...]))


def near(c, a, own, close):
    return pl.pallas_call(
        near_kernel,
        out_shape=jax.ShapeDtypeStruct(c.shape, jnp.float32),
        in_specs=[VMEM] * 4,
        out_specs=VMEM,
        compiler_params=pltpu.CompilerParams(vmem_limit_bytes=16 << 20),
        cost_estimate=pl.CostEstimate(flops=5 * 10**8, bytes_accessed=10**6, transcendentals=0),
    )(c, a, own, close)


def step_kernel(part_ref, b_ref, high_ref, low_ref, c_ref, projected_ref, ready_ref, out_ref):
    far = times(b_ref[...], high_ref[...], low_ref[...])
    out_ref[...] = update(part_ref[...] + far, c_ref[...], projected_ref[...], ready_ref[32:33, :])


def second_step_kernel(
    last, part_ref, other_ref, beyond_ref, high_ref, low_ref, c_ref, projected_ref, ready_ref, out_ref
):
    block = across(place())
    b = update(other_ref[0:16, :], other_ref[16:32, :], beyond_ref[...], other_ref[32:33, :])
    row = lax.broadcasted_iota(jnp.int32, b.shape, 0)
    b = jnp.where(row < jnp.where((block < 0) | (block > last), 0, 16), b, 0.0)
    far = times(b, high_ref[...], low_ref[...])
    out_ref[...] = update(part_ref[...] + far, c_ref[...], projected_ref[...], ready_ref[32:33, :])


def step(kernel, *operands):
    return pl.pallas_call(
        kernel,
        out_shape=jax.ShapeDtypeStruct(operands[0].shape, jnp.float32),
        in_specs=[VMEM] * len(operands),
        out_specs=VMEM,
        compiler_params=pltpu.CompilerParams(vmem_limit_bytes=16 << 20),
        cost_estimate=pl.CostEstimate(flops=3 * 10**8, bytes_accessed=10**6, transcendentals=0),
    )(*operands)


def swap_in_chip(c):
    n = lax.axis_size(AXES)
    return lax.ppermute(c, AXES, [(i, i ^ 1) for i in range(n)])


def swap_across(c):
    n = lax.axis_size(AXES)
    return lax.ppermute(c, AXES, [(i, across(i)) for i in range(1, n - 1)])


def local(
    movie,
    entry_tile,
    entry_neuron,
    entry_weights,
    intersection_self,
    intersection_prev,
    intersection_next,
    prev_traces,
):
    devices = lax.axis_size(AXES)
    matrices = (intersection_self, intersection_prev, intersection_next)
    c, _ = lax.optimization_barrier((prev_traces, opening()))
    a, b = swap_in_chip(c), swap_across(c)
    here = pltpu.with_memory_space_constraint(movie, pltpu.VMEM)
    send = contributions(here, entry_tile, entry_neuron, entry_weights, devices)
    got = lax.all_to_all(send.reshape(devices, 1, SLOT * LANES), AXES, 0, 0)
    ready, *split, close = prepare(c, a, b, matrices)
    other = swap_across(ready)
    got = got.reshape(devices * SLOT, LANES)
    projected, c = combine(first_kernel, got, ready, 2)
    a = swap_in_chip(c)
    beyond, = combine(beyond_kernel, got, projected, 1)
    part = near(c, a, intersection_self, close)
    second_step = functools.partial(second_step_kernel, devices - 1)
    c = step(second_step, part, other, beyond, *split, c, projected, ready)
    for _ in range(SWEEPS - 2):
        a, b = swap_in_chip(c), swap_across(c)
        part = near(c, a, intersection_self, close)
        c = step(step_kernel, part, b, *split, c, projected, ready)
    return c


def solution(mesh):
    return jax.shard_map(
        local,
        mesh=mesh,
        in_specs=(
            P(AXES, None),
            P(AXES),
            P(AXES),
            P(AXES, None),
            P(AXES, None),
            P(AXES, None),
            P(AXES, None),
            P(None, AXES),
        ),
        out_specs=P(None, AXES),
        check_vma=False,
    )
```
